256 devices in a mesh: dp: 2 (over z_lo), tensor: 128 (over x, y, z_hi, core).
Axes of the slice: x: 4, y: 4, z: 8 (z_hi: 4, z_lo: 2; z = z_hi * 2 + z_lo), core: 2. Of those that a mesh axis runs over, the one named last changes fastest.
Arguments:
- tokens: bfloat16 [2, 16384, 4096], P('dp', 'tensor'), may hold values from -35 to 35
- norm_gain: float32 [4096], replicated, may hold values from 0.1 to 1.9
- segments: int32 [2, 16384], P('dp', 'tensor'), may hold values from 0 to 7, never falling along the last dimension, each value on 1 to 8192 neighbouring positions
- deal_table: int32 [128, 2], P('tensor'), may hold values from 0 to 1, each once within a row
- projection: bfloat16 [32768, 768], P('tensor'), may hold values from -1 to 1
Outputs:
- context: bfloat16 [2, 16384, 4096], P('dp', 'tensor')
- key_cache: bfloat16 [2, 8, 16384, 128], P('dp', None, 'tensor')
- value_cache: bfloat16 [2, 8, 16384, 128], P('dp', None, 'tensor')
The draws below stay inside these ranges and needn't reach their ends.
Inputs may be any that keep to these rules, and one draw needn't show every extreme that they name: `segments`: segment ids never fall along a buffer; every id appears, each on at most 8192 positions, one on exactly 8192. `deal_table`: each row names every group once.
All inputs are finite; a program needn't handle non-finite values.
Results may differ from the reference program's by a relative error of at most 0.0082.
Values may be sent and summed in bfloat16 or wider, within the bound.
A program may use at most 128 MiB of HBM per device.

```python
import math
import jax
import jax.numpy as jnp
import numpy as np
from jax import lax

MODEL_DIMENSION = 4096
QUERY_HEADS = 32
KEY_VALUE_HEADS = 8
HEAD_SIZE = 128
TOK_DEV = 128
NSEG = 8
WINDOW = 512
SINKS = 4
QUERY_BLOCKS = 16
SLAB_FEATURES = 256
GROUP_TOKENS = 16384
MOST = 8192
HEAD_COLUMNS = 768
N_DP = 2
N_TENSOR = 128


def draw_tokens(key, part):
    body_key = jax.random.fold_in(key, 11)
    row_key = jax.random.fold_in(key, 12)
    column_key = jax.random.fold_in(key, 13)
    shape_full = (N_DP, GROUP_TOKENS, MODEL_DIMENSION)
    row_scale = jnp.exp(jax.random.uniform(row_key, (N_DP, GROUP_TOKENS, 1), jnp.float32, 0.0, math.log(10.0))) * 0.34
    column_scale = jnp.exp(jax.random.uniform(column_key, (1, 1, MODEL_DIMENSION), jnp.float32, 0.0, math.log(10.0))) * 0.34
    entries = jax.random.truncated_normal(body_key, -3.0, 3.0, shape_full, jnp.float32)
    return (entries * row_scale * column_scale).astype(jnp.bfloat16)


def draw_projection(key, part):
    first_key = jax.random.fold_in(key, 21)
    row_total = KEY_VALUE_HEADS * MODEL_DIMENSION
    base_draw = jax.random.truncated_normal(first_key, -3.0, 3.0, (row_total, HEAD_COLUMNS), jnp.float32)
    return jnp.clip(base_draw * MODEL_DIMENSION ** (-0.5), -1.0, 1.0).astype(jnp.bfloat16)


def profile(count, total, reach, lean):
    portions = [(1 << 20) // math.isqrt(standing ** lean) + 1 for standing in range(2, count + 1)]
    spare, given = total - reach - (count - 1), [1] * (count - 1)
    while spare > 0:
        movable = [i for i in range(count - 1) if given[i] < reach]
        mass, remaining = sum([portions[i] for i in movable]), spare
        for i in movable:
            more = min(reach - given[i], max(1, remaining * portions[i] // mass), spare)
            given[i] = given[i] + more
            spare = spare - more
    return np.array([reach] + given)


def uneven(key, amount, total, most, skew):
    if amount == 2:
        one = jax.random.randint(key, (), max(1, total - most), min(most, total - 1) + 1)
        return jnp.stack([one, total - one])
    lengths = jnp.asarray(profile(amount, total, most, skew), jnp.int32)
    pairs = (amount - 1) // 2
    giver, taker = lengths[1:1 + 2 * pairs:2], lengths[2:2 + 2 * pairs:2]
    slack = jnp.minimum(giver - 1, most - taker)
    passed = jax.random.randint(jax.random.fold_in(key, 1), (pairs,), 0, 1 << 20) % (slack + 1)
    lengths = lengths.at[1:1 + 2 * pairs:2].set(giver - passed).at[2:2 + 2 * pairs:2].set(taker + passed)
    return lengths[jax.random.permutation(jax.random.fold_in(key, 2), amount)]


def setup_inputs(seed: int = 0) -> dict:
    streams_of = jax.random.split(jax.random.key(seed), 6)
    tokens = draw_tokens(jax.random.fold_in(streams_of[5], 71), 0)
    norm_gain = jnp.clip(1.0 + 0.18 * jax.random.normal(streams_of[1], (MODEL_DIMENSION,), jnp.float32), 0.1, 1.9)
    segments = jax.vmap(lambda own: jnp.searchsorted(jnp.cumsum(uneven(own, NSEG, GROUP_TOKENS, MOST, 2)), jnp.arange(GROUP_TOKENS), side="right"))(jax.random.split(streams_of[2], N_DP)).reshape((N_DP, GROUP_TOKENS)).astype(jnp.int32)
    deal_table = jax.vmap(lambda own: jax.random.permutation(own, N_DP))(jax.random.split(streams_of[3], N_TENSOR)).reshape((N_TENSOR, N_DP)).astype(jnp.int32)
    projection = draw_projection(jax.random.fold_in(streams_of[5], 71), 0)
    return dict(tokens=tokens, norm_gain=norm_gain, segments=segments, deal_table=deal_table, projection=projection)


rope_base = 500000.0
norm_eps = 1e-05

def rotary(values, angles):
    half_width = values.shape[-1] // 2
    first_half = values[..., :half_width]
    second_half = values[..., half_width:]
    cosine = jnp.cos(angles)
    sine_part = jnp.sin(angles)
    return jnp.concatenate((first_half * cosine - second_half * sine_part, second_half * cosine + first_half * sine_part), -1)

def attend_group(query_rows, key_rows, value_rows, row_starts):
    tile_rows = math.gcd(GROUP_TOKENS, 512)
    pad_block = jnp.zeros((WINDOW, HEAD_SIZE), jnp.bfloat16)
    keys_padded = jnp.concatenate((pad_block, key_rows), 0)
    values_padded = jnp.concatenate((pad_block, value_rows), 0)
    score_scale = HEAD_SIZE ** (-0.5)

    def single_tile(tile_start):
        query_tile = lax.dynamic_slice_in_dim(query_rows, tile_start, tile_rows, 0).astype(jnp.float32)
        query_pos = tile_start + jnp.arange(tile_rows, dtype=jnp.int32)
        query_start = lax.dynamic_slice_in_dim(row_starts, tile_start, tile_rows, 0)
        key_tile = lax.dynamic_slice_in_dim(keys_padded, tile_start, WINDOW + tile_rows, 0).astype(jnp.float32)
        value_tile = lax.dynamic_slice_in_dim(values_padded, tile_start, WINDOW + tile_rows, 0).astype(jnp.float32)
        key_pos = tile_start - WINDOW + jnp.arange(WINDOW + tile_rows, dtype=jnp.int32)
        scores = jnp.einsum('rgd,kd->rgk', query_tile, key_tile) * score_scale
        allowed = (key_pos[None, :] <= query_pos[:, None]) & (key_pos[None, :] >= query_start[:, None]) & (key_pos[None, :] >= query_pos[:, None] - WINDOW)
        sink_pos = query_start[:, None] + jnp.arange(SINKS, dtype=jnp.int32)[None, :]
        sink_index = jnp.minimum(sink_pos, GROUP_TOKENS - 1).astype(jnp.int32)
        sink_keys = key_rows[sink_index].astype(jnp.float32)
        sink_values = value_rows[sink_index].astype(jnp.float32)
        sink_scores = jnp.einsum('rgd,rqd->rgq', query_tile, sink_keys) * score_scale
        sink_allowed = (sink_pos <= query_pos[:, None]) & (sink_pos < query_pos[:, None] - WINDOW)
        masked = jnp.where(allowed[:, None, :], scores, -jnp.inf)
        masked_sinks = jnp.where(sink_allowed[:, None, :], sink_scores, -jnp.inf)
        top_score = jnp.maximum(lax.optimization_barrier(jnp.max(masked, -1, keepdims=True)), lax.optimization_barrier(jnp.max(masked_sinks, -1, keepdims=True)))
        window_weights = jnp.exp(masked - top_score)
        sink_weights = jnp.exp(masked_sinks - top_score)
        denominator = lax.optimization_barrier(jnp.sum(window_weights, -1, keepdims=True)) + lax.optimization_barrier(jnp.sum(sink_weights, -1, keepdims=True))
        window_probs = lax.optimization_barrier((window_weights / denominator).astype(jnp.bfloat16)).astype(jnp.float32)
        sink_probs = lax.optimization_barrier((sink_weights / denominator).astype(jnp.bfloat16)).astype(jnp.float32)
        mixed_rows = jnp.einsum('rgk,kd->rgd', window_probs, value_tile)
        mixed_rows = mixed_rows + jnp.einsum('rgq,rqd->rgd', sink_probs, sink_values)
        return mixed_rows.astype(jnp.bfloat16)
    tile_offsets = jnp.arange(GROUP_TOKENS // tile_rows, dtype=jnp.int32) * tile_rows
    return lax.map(single_tile, tile_offsets).reshape(GROUP_TOKENS, QUERY_HEADS // KEY_VALUE_HEADS * HEAD_SIZE)

def reference(tokens, norm_gain, segments, deal_table, projection):
    group_queries = QUERY_HEADS // KEY_VALUE_HEADS
    page_blocks = tokens.reshape(N_DP, N_TENSOR, TOK_DEV, MODEL_DIMENSION)
    weight_params = projection.reshape(QUERY_BLOCKS, KEY_VALUE_HEADS, SLAB_FEATURES, HEAD_COLUMNS).transpose(1, 0, 2, 3).reshape(KEY_VALUE_HEADS, MODEL_DIMENSION, HEAD_COLUMNS)
    rope_freq = rope_base ** (-(jnp.arange(0, HEAD_SIZE, 2).astype(jnp.float32) / HEAD_SIZE))
    contexts = []
    key_groups = []
    value_groups = []
    for target in range(N_DP):
        dealt_rows = jnp.zeros((N_TENSOR, TOK_DEV, MODEL_DIMENSION), jnp.bfloat16)
        for source in range(N_DP):
            dealt_rows = jnp.where((deal_table[:, source] == target)[:, None, None], page_blocks[source], dealt_rows)
        widened = dealt_rows.reshape(GROUP_TOKENS, MODEL_DIMENSION).astype(jnp.float32)
        normed = (widened * lax.rsqrt(lax.optimization_barrier(jnp.mean(widened * widened, -1, keepdims=True)) + norm_eps) * norm_gain).astype(jnp.bfloat16)
        segment_ids = segments[target]
        counts = lax.optimization_barrier(jnp.sum((segment_ids[:, None] == jnp.arange(NSEG, dtype=jnp.int32)[None, :]).astype(jnp.int32), 0)).astype(jnp.int32)
        seg_starts = (jnp.cumsum(counts) - counts).astype(jnp.int32)
        row_starts = seg_starts[segment_ids].astype(jnp.int32)
        angles = (jnp.arange(GROUP_TOKENS, dtype=jnp.int32) - row_starts).astype(jnp.float32)[:, None] * rope_freq[None, :]
        context_heads = []
        key_heads = []
        value_heads = []
        for head_number in range(KEY_VALUE_HEADS):
            projected = jnp.dot(normed, weight_params[head_number], preferred_element_type=jnp.float32)
            query_rows = rotary(projected[:, :group_queries * HEAD_SIZE].reshape(GROUP_TOKENS, group_queries, HEAD_SIZE), angles[:, None, :]).astype(jnp.bfloat16)
            key_rows = rotary(projected[:, group_queries * HEAD_SIZE:(group_queries + 1) * HEAD_SIZE], angles).astype(jnp.bfloat16)
            value_rows = projected[:, (group_queries + 1) * HEAD_SIZE:].astype(jnp.bfloat16)
            context_heads.append(attend_group(query_rows, key_rows, value_rows, row_starts))
            key_heads.append(key_rows)
            value_heads.append(value_rows)
        contexts.append(jnp.concatenate(context_heads, 1))
        key_groups.append(jnp.stack(key_heads))
        value_groups.append(jnp.stack(value_heads))
    context_groups = jnp.stack(contexts).reshape(N_DP, N_TENSOR, TOK_DEV, QUERY_HEADS * HEAD_SIZE)
    returned = []
    for client in range(N_DP):
        collected = jnp.zeros((N_TENSOR, TOK_DEV, QUERY_HEADS * HEAD_SIZE), jnp.bfloat16)
        for target in range(N_DP):
            collected = jnp.where((deal_table[:, client] == target)[:, None, None], context_groups[target], collected)
        returned.append(collected.reshape(GROUP_TOKENS, QUERY_HEADS * HEAD_SIZE))
    return (jnp.stack(returned), jnp.stack(key_groups), jnp.stack(value_groups))
```

```python
import jax
import jax.numpy as jnp
from jax import lax
from jax.sharding import PartitionSpec as P

QUERY_HEADS = 32
KEY_VALUE_HEADS = 8
HEAD_SIZE = 128
NSEG = 8
WINDOW = 512
SINKS = 4


rope_base = 500000.0
norm_eps = 1e-05


def from_partner(value, axis, apart):
    mask = 2**apart
    pairs = [(source, source ^ mask) for source in range(lax.axis_size(axis))]
    return lax.ppermute(value, axis, pairs)


def shifted(block, axis, distance):
    devices = range(lax.axis_size(axis))
    route = [(i - distance, i) for i in devices if i - distance in devices]
    return lax.ppermute(block, axis, route)


def stack_pair(holding, arrived, upper_flag, axis_pos):
    lower_part = jnp.where(upper_flag, arrived, holding)
    upper_part = jnp.where(upper_flag, holding, arrived)
    return jnp.stack((lower_part, upper_part), axis=axis_pos)


def rotary(values, angles):
    half_width = values.shape[-1] // 2
    first_half = values[..., :half_width]
    second_half = values[..., half_width:]
    cosine = jnp.cos(angles)
    sine_part = jnp.sin(angles)
    return jnp.concatenate(
        (
            first_half * cosine - second_half * sine_part,
            second_half * cosine + first_half * sine_part,
        ),
        -1,
    )


def body(tokens, norm_gain, segments, deal_table, projection):
    group_id = lax.axis_index("dp")
    device_number = lax.axis_index("tensor")
    tensor_width = lax.axis_size("tensor")
    token_per_device = tokens.shape[1]
    model_width = tokens.shape[2]
    block_length = KEY_VALUE_HEADS * token_per_device
    block_number = device_number // KEY_VALUE_HEADS
    group_queries = QUERY_HEADS // KEY_VALUE_HEADS
    head_bit_flags = KEY_VALUE_HEADS.bit_length() - 1
    level_bits = tensor_width.bit_length() - 1
    own_page = tokens[0]
    other_page = from_partner(own_page, "dp", 0)
    owner_group = jnp.sum(jnp.where(jnp.arange(deal_table.shape[1]) == group_id, deal_table[0], 0))
    stay_here = owner_group == group_id
    dealt_rows = jnp.where(stay_here, own_page, other_page)
    widened = dealt_rows.astype(jnp.float32)
    normed = (
        widened * lax.rsqrt(jnp.mean(widened * widened, -1, keepdims=True) + norm_eps) * norm_gain
    ).astype(jnp.bfloat16)
    segment_ids = segments[0]
    bit_order = list(range(head_bit_flags))
    rows_held = normed
    starts_held = segment_ids
    gathered_bits = []
    for bit_index in bit_order:
        upper_flag = device_number >> bit_index & 1 == 1
        axis_pos = len([earlier for earlier in gathered_bits if earlier > bit_index])
        rows_far = from_partner(rows_held, "tensor", bit_index)
        starts_far = from_partner(starts_held, "tensor", bit_index)
        rows_held = stack_pair(rows_held, rows_far, upper_flag, axis_pos)
        starts_held = stack_pair(starts_held, starts_far, upper_flag, axis_pos)
        gathered_bits.append(bit_index)
    rows_block = rows_held.reshape(block_length, model_width)
    segments_block = starts_held.reshape(block_length)
    segment_match = segments_block[:, None] == jnp.arange(NSEG)[None, :]
    counts_int = jnp.sum(segment_match.astype(jnp.int32), 0)
    for bit_index in range(head_bit_flags, level_bits):
        counts_int = counts_int + from_partner(counts_int, "tensor", bit_index)
    seg_starts = jnp.cumsum(counts_int) - counts_int
    starts_block = jnp.sum(jnp.where(segment_match, seg_starts[None, :], 0), 1)
    weights_held = projection
    for level_index in range(level_bits - head_bit_flags):
        bit_index = head_bit_flags + level_index
        upper_flag = device_number >> bit_index & 1 == 1
        arrived = from_partner(weights_held, "tensor", bit_index)
        weights_held = stack_pair(weights_held, arrived, upper_flag, 0).reshape(
            -1, weights_held.shape[1]
        )
    projected = jnp.dot(rows_block, weights_held, preferred_element_type=jnp.float32)
    rope_freq = rope_base ** (-(jnp.arange(0, HEAD_SIZE, 2).astype(jnp.float32) / HEAD_SIZE))
    block_positions = block_number * block_length + jnp.arange(block_length)
    angles = (block_positions - starts_block).astype(jnp.float32)[:, None] * rope_freq[None, :]
    queries = rotary(
        projected[:, : group_queries * HEAD_SIZE].reshape(block_length, group_queries, HEAD_SIZE),
        angles[:, None, :],
    ).astype(jnp.bfloat16)
    keys_own = rotary(
        projected[:, group_queries * HEAD_SIZE : (group_queries + 1) * HEAD_SIZE], angles
    ).astype(jnp.bfloat16)
    values_own = projected[:, (group_queries + 1) * HEAD_SIZE :].astype(jnp.bfloat16)
    local_pairs = jnp.concatenate((keys_own, values_own), 1)
    reach_blocks = -(-WINDOW // block_length)
    previous_pairs = [shifted(local_pairs, "tensor", 1 * KEY_VALUE_HEADS)]
    window_pairs = jnp.concatenate(previous_pairs + [local_pairs], 0)
    sink_positions = (seg_starts[:, None] + jnp.arange(SINKS)[None, :]).reshape(NSEG * SINKS)
    local_rows = sink_positions - block_number * block_length
    selector = (local_rows[:, None] == jnp.arange(block_length)[None, :]).astype(jnp.bfloat16)
    sink_flat = jnp.dot(selector, local_pairs, preferred_element_type=jnp.float32).astype(
        jnp.bfloat16
    )
    for bit_index in range(head_bit_flags, level_bits):
        sink_flat = sink_flat + from_partner(sink_flat, "tensor", bit_index)
    sink_pairs = sink_flat.reshape(NSEG, SINKS, 2 * HEAD_SIZE)
    tile_rows = min(512, block_length)
    score_scale = HEAD_SIZE ** (-0.5)

    def attend(tile_start):
        query_tile = lax.dynamic_slice_in_dim(queries, tile_start, tile_rows, 0)
        query_pos = block_number * block_length + tile_start + jnp.arange(tile_rows)
        query_start = lax.dynamic_slice_in_dim(starts_block, tile_start, tile_rows, 0)
        key_from = reach_blocks * block_length + tile_start - WINDOW
        key_pairs = lax.dynamic_slice_in_dim(window_pairs, key_from, WINDOW + tile_rows, 0)
        key_pos = (
            (block_number - reach_blocks) * block_length + key_from + jnp.arange(WINDOW + tile_rows)
        )
        scores = (
            jnp.einsum(
                "rgd,kd->rgk",
                query_tile,
                key_pairs[:, :HEAD_SIZE],
                preferred_element_type=jnp.float32,
            )
            * score_scale
        )
        allowed = (
            (key_pos[None, :] <= query_pos[:, None])
            & (key_pos[None, :] >= query_start[:, None])
            & (key_pos[None, :] >= query_pos[:, None] - WINDOW)
        )
        chooser = (seg_starts[None, :] == query_start[:, None]).astype(jnp.bfloat16)
        row_sinks = jnp.einsum(
            "rs,sqc->rqc", chooser, sink_pairs, preferred_element_type=jnp.float32
        ).astype(jnp.bfloat16)
        sink_scores = (
            jnp.einsum(
                "rgd,rqd->rgq",
                query_tile,
                row_sinks[:, :, :HEAD_SIZE],
                preferred_element_type=jnp.float32,
            )
            * score_scale
        )
        sink_pos = query_start[:, None] + jnp.arange(SINKS)[None, :]
        sink_allowed = (sink_pos <= query_pos[:, None]) & (sink_pos < query_pos[:, None] - WINDOW)
        masked = jnp.where(allowed[:, None, :], scores, -jnp.inf)
        masked_sinks = jnp.where(sink_allowed[:, None, :], sink_scores, -jnp.inf)
        top_score = jnp.maximum(
            jnp.max(masked, -1, keepdims=True), jnp.max(masked_sinks, -1, keepdims=True)
        )
        window_weights = jnp.exp(masked - top_score)
        sink_weights = jnp.exp(masked_sinks - top_score)
        denominator = jnp.sum(window_weights, -1, keepdims=True) + jnp.sum(
            sink_weights, -1, keepdims=True
        )
        window_probs = (window_weights / denominator).astype(jnp.bfloat16)
        sink_probs = (sink_weights / denominator).astype(jnp.bfloat16)
        mixed_rows = jnp.einsum(
            "rgk,kd->rgd",
            window_probs,
            key_pairs[:, HEAD_SIZE:],
            preferred_element_type=jnp.float32,
        )
        mixed_rows = mixed_rows + jnp.einsum(
            "rgq,rqd->rgd",
            sink_probs,
            row_sinks[:, :, HEAD_SIZE:],
            preferred_element_type=jnp.float32,
        )
        return mixed_rows.astype(jnp.bfloat16).reshape(tile_rows, group_queries * HEAD_SIZE)

    tile_offsets = jnp.arange(block_length // tile_rows, dtype=jnp.int32) * tile_rows
    context_block = lax.map(attend, tile_offsets).reshape(block_length, group_queries * HEAD_SIZE)
    pairs_by_dest = local_pairs.reshape((2,) * head_bit_flags + (token_per_device, 2 * HEAD_SIZE))
    context_by_dest = context_block.reshape(
        (2,) * head_bit_flags + (token_per_device, group_queries * HEAD_SIZE)
    )
    kept_pairs = pairs_by_dest
    for bit_index in range(head_bit_flags):
        axis_pos = head_bit_flags - 1 - bit_index
        bit_value = device_number >> bit_index & 1
        own_half = lax.dynamic_index_in_dim(kept_pairs, bit_value, axis_pos, keepdims=False)
        sent_half = lax.dynamic_index_in_dim(kept_pairs, 1 - bit_value, axis_pos, keepdims=False)
        arrived = from_partner(sent_half, "tensor", bit_index)
        kept_pairs = stack_pair(own_half, arrived, bit_value == 1, axis_pos)
    kept_context = context_by_dest
    for bit_index in range(head_bit_flags):
        axis_pos = head_bit_flags - 1 - bit_index
        bit_value = device_number >> bit_index & 1
        own_half = lax.dynamic_index_in_dim(kept_context, bit_value, axis_pos, keepdims=False)
        sent_half = lax.dynamic_index_in_dim(kept_context, 1 - bit_value, axis_pos, keepdims=False)
        arrived = from_partner(sent_half, "tensor", bit_index)
        kept_context = stack_pair(own_half, arrived, bit_value == 1, axis_pos)
    cached_heads = kept_pairs.reshape(KEY_VALUE_HEADS, token_per_device, 2 * HEAD_SIZE)
    key_cache = cached_heads[:, :, :HEAD_SIZE][None]
    value_cache = cached_heads[:, :, HEAD_SIZE:][None]
    context_local = (
        kept_context.reshape(KEY_VALUE_HEADS, token_per_device, group_queries * HEAD_SIZE)
        .transpose(1, 0, 2)
        .reshape(token_per_device, QUERY_HEADS * HEAD_SIZE)
    )
    context_back = from_partner(context_local, "dp", 0)
    context = jnp.where(stay_here, context_local, context_back)[None]
    return (context, key_cache, value_cache)


def solution(mesh):
    placed = (P("dp", "tensor", None), P(), P("dp", "tensor"), P("tensor", None), P("tensor", None))
    return jax.shard_map(
        body,
        mesh=mesh,
        in_specs=placed,
        out_specs=(
            P("dp", "tensor", None),
            P("dp", None, "tensor", None),
            P("dp", None, "tensor", None),
        ),
        check_vma=False,
    )
```

```python
import jax
import jax.numpy as jnp
from jax import lax
from jax.experimental import pallas as pl
from jax.experimental.pallas import tpu as pltpu
from jax.sharding import PartitionSpec as P

QUERY_HEADS = 32
KEY_VALUE_HEADS = 8
HEAD_SIZE = 128
NSEG = 8
WINDOW = 512
SINKS = 4


rope_base = 500000.0
norm_eps = 1e-05


def from_partner(value, axis, apart):
    mask = 2**apart
    pairs = [(source, source ^ mask) for source in range(lax.axis_size(axis))]
    return lax.ppermute(value, axis, pairs)


def shifted(block, axis, distance):
    devices = range(lax.axis_size(axis))
    route = [(i - distance, i) for i in devices if i - distance in devices]
    return lax.ppermute(block, axis, route)


def stack_pair(holding, arrived, upper_flag, axis_pos):
    lower_part = jnp.where(upper_flag, arrived, holding)
    upper_part = jnp.where(upper_flag, holding, arrived)
    return jnp.stack((lower_part, upper_part), axis=axis_pos)


def rotary(values, angles):
    half_width = values.shape[-1] // 2
    first_half = values[..., :half_width]
    second_half = values[..., half_width:]
    cosine = jnp.cos(angles)
    sine_part = jnp.sin(angles)
    return jnp.concatenate(
        (
            first_half * cosine - second_half * sine_part,
            second_half * cosine + first_half * sine_part,
        ),
        -1,
    )


def gather_kernel(page, slab, note, pages, weights, notes, send, recv, local):
    dp = lax.axis_index("dp")
    t = lax.axis_index("tensor")
    core, zh = t % 2, (t // 2) % 4
    y, x = (t // 8) % 4, t // 32
    z = zh * 2 + dp
    q = t % 8

    def device(dx, dy, z_at, core_at):
        z_at = z_at % 8
        block = ((x + dx) % 4) * 4 + (y + dy) % 4
        return (z_at % 2, (block * 4 + z_at // 2) * 2 + core_at)

    slots = {}

    def copy(key, src, dst, target):
        i = slots.setdefault(key, len(slots))
        return pltpu.make_async_remote_copy(
            src_ref=src,
            dst_ref=dst,
            send_sem=send.at[i],
            recv_sem=recv.at[i],
            device_id=target,
            device_id_type=pl.DeviceIdType.MESH,
        )

    started = []

    def start(key, src, dst, target):
        c = copy(key, src, dst, target)
        c.start()
        started.append(c)

    partner = (dp, t + 1 - 2 * core)

    def arrived(key, dst):
        copy(key, dst, dst, partner).wait_recv()

    group = [(dp, (t // 8) * 8 + (q + r) % 8) for r in range(1, 8)]
    columns = [device(r, 0, z, core) for r in range(1, 4)]
    lines = [device(0, r, z, core) for r in range(1, 4)]
    ring = {1: device(0, 0, z + 1, core), -1: device(0, 0, z + 7, core)}
    barrier = pltpu.get_barrier_semaphore()
    peers = group + columns + lines + [ring[1], ring[-1]]
    for peer in peers:
        pl.semaphore_signal(barrier, inc=1, device_id=peer, device_id_type=pl.DeviceIdType.MESH)
    pl.semaphore_wait(barrier, len(peers))

    def page_at(dz, h, c):
        return pages.at[(z + dz + 8) % 8, c, h]

    def origin(order, da, db):
        dx, dy = (da, db) if order == 0 else (db, da)
        return weights.at[((x + dx + 4) % 4) * 4 + (y + dy + 4) % 4, order]

    def towards(order, da, db):
        dx, dy = (da, db) if order == 0 else (db, da)
        return device(dx + 4, dy + 4, z, core)

    own_copies = [
        pltpu.make_async_copy(page, pages.at[z, core], local.at[0]),
        pltpu.make_async_copy(slab, weights.at[x * 4 + y], local.at[1]),
        pltpu.make_async_copy(note, notes.at[y, x, q], local.at[2]),
    ]
    for c in own_copies:
        c.start()
    for r in range(1, 8):
        start(("note", r), note, notes.at[y, x, q], group[r - 1])
    for order in range(2):
        for d in (1, -1):
            start(("w1", order, d), slab.at[order], origin(order, 0, 0), towards(order, d, 0))
    for h in range(2):
        for d in (1, -1):
            start(("z", d, 0, h), page.at[h], page_at(0, h, core), ring[d])
    for order in range(2):
        for d in (1, -1):
            start(("w2", order, 0, d), slab.at[order], origin(order, 0, 0), towards(order, 0, d))
    for h in range(2):
        start(("c", 0, 0, h), page.at[h], page_at(0, h, core), partner)

    def page_step(s, h):
        for d in (1, -1):
            if s == 3 and h != (0 if d == 1 else 1):
                continue
            at = page_at(-d * (s + 1), h, core)
            arrived(("z", d, s, h), at)
            if s + 1 < 3 or (s + 1 == 3 and h == (0 if d == 1 else 1)):
                start(("z", d, s + 1, h), at, at, ring[d])
            start(("c", d, s, h), at, at, partner)

    def second_send(order, k):
        for d in (1, -1):
            start(("w2", order, k, d), origin(order, k, 0), origin(order, k, 0), towards(order, 0, d))

    def second_relay(order, k):
        for d in (1, -1):
            at = origin(order, k, -d)
            arrived(("w2", order, k, d), at)
            half = at.at[0 if d == 1 else 1]
            start(("w2r", order, k, d), half, half, towards(order, 0, d))

    for r in range(1, 8):
        arrived(("note", r), notes.at[y, x, (q + 8 - r) % 8])
    own_copies[2].wait()
    for r in range(1, 4):
        start(("notex", r), notes.at[y, x], notes.at[y, x], columns[r - 1])
    for order in range(2):
        for d in (1, -1):
            at = origin(order, -d, 0)
            arrived(("w1", order, d), at)
            half = at.at[0 if d == 1 else 1]
            start(("w1r", order, d), half, half, towards(order, d, 0))
            second_send(order, -d)
    for order in range(2):
        second_relay(order, 0)
    for r in range(1, 4):
        arrived(("notex", r), notes.at[y, (x + 4 - r) % 4])
    for r in range(1, 4):
        start(("notey", r), notes.at[y], notes.at[y], lines[r - 1])
    page_step(0, 0)
    for order in range(2):
        for d in (1, -1):
            arrived(("w1r", order, d), origin(order, -2 * d, 0).at[0 if d == 1 else 1])
        second_send(order, 2)
    for order in range(2):
        second_relay(order, -1)
        second_relay(order, 1)
    page_step(0, 1)
    for order in range(2):
        second_relay(order, 2)
    page_step(1, 0)
    for r in range(1, 4):
        arrived(("notey", r), notes.at[(y + 4 - r) % 4])
    for order in range(2):
        for k in (0, -1, 1, 2):
            for d in (1, -1):
                arrived(("w2r", order, k, d), origin(order, k, -2 * d).at[0 if d == 1 else 1])
    page_step(1, 1)
    for s, h in ((2, 0), (2, 1), (3, 0), (3, 1)):
        page_step(s, h)
    for h in range(2):
        arrived(("c", 0, 0, h), page_at(0, h, 1 - core))
    for s in range(4):
        for h in range(2):
            for d in (1, -1):
                if s < 3 or h == (0 if d == 1 else 1):
                    arrived(("c", d, s, h), page_at(-d * (s + 1), h, 1 - core))
    for c in started:
        c.wait_send()
    own_copies[0].wait()
    own_copies[1].wait()


COPIES = 7 + 3 + 3 + 14 + 16 + 4 + 4 + 16 + 16


def gather(page, slab, note):
    rows, width = page.shape
    depth, columns = slab.shape
    vmem = pl.BlockSpec(memory_space=pltpu.VMEM)
    hbm = pl.BlockSpec(memory_space=pltpu.HBM)
    return pl.pallas_call(
        gather_kernel,
        out_shape=(
            jax.ShapeDtypeStruct((8, 2, 2, rows // 2, width), page.dtype),
            jax.ShapeDtypeStruct((16, 2, 2, depth // 4, columns), slab.dtype),
            jax.ShapeDtypeStruct((4, 4, 8, 1, note.shape[0]), note.dtype),
        ),
        in_specs=[vmem] * 3,
        out_specs=(hbm,) * 3,
        scratch_shapes=[
            pltpu.SemaphoreType.DMA((COPIES,)),
            pltpu.SemaphoreType.DMA((COPIES,)),
            pltpu.SemaphoreType.DMA((3,)),
        ],
        compiler_params=pltpu.CompilerParams(collective_id=0, has_side_effects=True),
        name="gather",
    )(
        page.reshape(2, rows // 2, width),
        slab.reshape(2, 2, depth // 4, columns),
        note.reshape(1, -1),
    )


def body(tokens, norm_gain, segments, deal_table, projection):
    group_id = lax.axis_index("dp")
    device_number = lax.axis_index("tensor")
    tensor_width = lax.axis_size("tensor")
    token_per_device = tokens.shape[1]
    model_width = tokens.shape[2]
    block_length = KEY_VALUE_HEADS * token_per_device
    block_number = device_number // KEY_VALUE_HEADS
    group_queries = QUERY_HEADS // KEY_VALUE_HEADS
    head_bit_flags = KEY_VALUE_HEADS.bit_length() - 1
    level_bits = tensor_width.bit_length() - 1
    own_page = tokens[0]
    owner_group = jnp.sum(jnp.where(jnp.arange(deal_table.shape[1]) == group_id, deal_table[0], 0))
    stay_here = owner_group == group_id
    widened = own_page.astype(jnp.float32)
    normed = (
        widened * lax.rsqrt(jnp.mean(widened * widened, -1, keepdims=True) + norm_eps) * norm_gain
    ).astype(jnp.bfloat16)
    client = jnp.where(stay_here, group_id, 1 - group_id).astype(jnp.int32)
    note = jnp.concatenate((segments[0], jnp.broadcast_to(client, segments[0].shape)))
    pages, weights, notes = gather(normed, projection, note)
    weights_held = weights.reshape(model_width, projection.shape[1])
    notes = notes.reshape(4, 4, KEY_VALUE_HEADS, 2, token_per_device).transpose(1, 0, 2, 3, 4)
    notes = notes.reshape(-1, KEY_VALUE_HEADS, 2, token_per_device)
    counts_int = jnp.sum(
        (notes[:, :, 0, :, None] == jnp.arange(NSEG)).astype(jnp.int32), (0, 1, 2)
    )
    seg_starts = jnp.cumsum(counts_int) - counts_int
    own_notes = lax.dynamic_index_in_dim(notes, block_number, 0, keepdims=False)
    segment_match = own_notes[:, 0].reshape(block_length)[:, None] == jnp.arange(NSEG)[None, :]
    starts_block = jnp.sum(jnp.where(segment_match, seg_starts[None, :], 0), 1)
    clients = own_notes[:, 1, 0].reshape(4, 2, 1, 1)
    pages = pages.reshape(4, 2, 2, token_per_device, model_width)
    rows_block = jnp.where(clients == 1, pages[:, 1], pages[:, 0]).reshape(
        block_length, model_width
    )
    projected = jnp.dot(rows_block, weights_held, preferred_element_type=jnp.float32)
    rope_freq = rope_base ** (-(jnp.arange(0, HEAD_SIZE, 2).astype(jnp.float32) / HEAD_SIZE))
    block_positions = block_number * block_length + jnp.arange(block_length)
    angles = (block_positions - starts_block).astype(jnp.float32)[:, None] * rope_freq[None, :]
    queries = rotary(
        projected[:, : group_queries * HEAD_SIZE].reshape(block_length, group_queries, HEAD_SIZE),
        angles[:, None, :],
    ).astype(jnp.bfloat16)
    keys_own = rotary(
        projected[:, group_queries * HEAD_SIZE : (group_queries + 1) * HEAD_SIZE], angles
    ).astype(jnp.bfloat16)
    values_own = projected[:, (group_queries + 1) * HEAD_SIZE :].astype(jnp.bfloat16)
    local_pairs = jnp.concatenate((keys_own, values_own), 1)
    reach_blocks = -(-WINDOW // block_length)
    previous_pairs = [shifted(local_pairs, "tensor", 1 * KEY_VALUE_HEADS)]
    window_pairs = jnp.concatenate(previous_pairs + [local_pairs], 0)
    sink_positions = (seg_starts[:, None] + jnp.arange(SINKS)[None, :]).reshape(NSEG * SINKS)
    local_rows = sink_positions - block_number * block_length
    selector = (local_rows[:, None] == jnp.arange(block_length)[None, :]).astype(jnp.bfloat16)
    sink_flat = jnp.dot(selector, local_pairs, preferred_element_type=jnp.float32).astype(
        jnp.bfloat16
    )
    for bit_index in range(head_bit_flags, level_bits):
        sink_flat = sink_flat + from_partner(sink_flat, "tensor", bit_index)
    sink_pairs = sink_flat.reshape(NSEG, SINKS, 2 * HEAD_SIZE)
    tile_rows = min(512, block_length)
    score_scale = HEAD_SIZE ** (-0.5)

    def attend(tile_start):
        query_tile = lax.dynamic_slice_in_dim(queries, tile_start, tile_rows, 0)
        query_pos = block_number * block_length + tile_start + jnp.arange(tile_rows)
        query_start = lax.dynamic_slice_in_dim(starts_block, tile_start, tile_rows, 0)
        key_from = reach_blocks * block_length + tile_start - WINDOW
        key_pairs = lax.dynamic_slice_in_dim(window_pairs, key_from, WINDOW + tile_rows, 0)
        key_pos = (
            (block_number - reach_blocks) * block_length + key_from + jnp.arange(WINDOW + tile_rows)
        )
        scores = (
            jnp.einsum(
                "rgd,kd->rgk",
                query_tile,
                key_pairs[:, :HEAD_SIZE],
                preferred_element_type=jnp.float32,
            )
            * score_scale
        )
        allowed = (
            (key_pos[None, :] <= query_pos[:, None])
            & (key_pos[None, :] >= query_start[:, None])
            & (key_pos[None, :] >= query_pos[:, None] - WINDOW)
        )
        chooser = (seg_starts[None, :] == query_start[:, None]).astype(jnp.bfloat16)
        row_sinks = jnp.einsum(
            "rs,sqc->rqc", chooser, sink_pairs, preferred_element_type=jnp.float32
        ).astype(jnp.bfloat16)
        sink_scores = (
            jnp.einsum(
                "rgd,rqd->rgq",
                query_tile,
                row_sinks[:, :, :HEAD_SIZE],
                preferred_element_type=jnp.float32,
            )
            * score_scale
        )
        sink_pos = query_start[:, None] + jnp.arange(SINKS)[None, :]
        sink_allowed = (sink_pos <= query_pos[:, None]) & (sink_pos < query_pos[:, None] - WINDOW)
        masked = jnp.where(allowed[:, None, :], scores, -jnp.inf)
        masked_sinks = jnp.where(sink_allowed[:, None, :], sink_scores, -jnp.inf)
        top_score = jnp.maximum(
            jnp.max(masked, -1, keepdims=True), jnp.max(masked_sinks, -1, keepdims=True)
        )
        window_weights = jnp.exp(masked - top_score)
        sink_weights = jnp.exp(masked_sinks - top_score)
        denominator = jnp.sum(window_weights, -1, keepdims=True) + jnp.sum(
            sink_weights, -1, keepdims=True
        )
        window_probs = (window_weights / denominator).astype(jnp.bfloat16)
        sink_probs = (sink_weights / denominator).astype(jnp.bfloat16)
        mixed_rows = jnp.einsum(
            "rgk,kd->rgd",
            window_probs,
            key_pairs[:, HEAD_SIZE:],
            preferred_element_type=jnp.float32,
        )
        mixed_rows = mixed_rows + jnp.einsum(
            "rgq,rqd->rgd",
            sink_probs,
            row_sinks[:, :, HEAD_SIZE:],
            preferred_element_type=jnp.float32,
        )
        return mixed_rows.astype(jnp.bfloat16).reshape(tile_rows, group_queries * HEAD_SIZE)

    tile_offsets = jnp.arange(block_length // tile_rows, dtype=jnp.int32) * tile_rows
    context_block = lax.map(attend, tile_offsets).reshape(block_length, group_queries * HEAD_SIZE)
    pairs_by_dest = local_pairs.reshape((2,) * head_bit_flags + (token_per_device, 2 * HEAD_SIZE))
    context_by_dest = context_block.reshape(
        (2,) * head_bit_flags + (token_per_device, group_queries * HEAD_SIZE)
    )
    kept_pairs = pairs_by_dest
    for bit_index in range(head_bit_flags):
        axis_pos = head_bit_flags - 1 - bit_index
        bit_value = device_number >> bit_index & 1
        own_half = lax.dynamic_index_in_dim(kept_pairs, bit_value, axis_pos, keepdims=False)
        sent_half = lax.dynamic_index_in_dim(kept_pairs, 1 - bit_value, axis_pos, keepdims=False)
        arrived = from_partner(sent_half, "tensor", bit_index)
        kept_pairs = stack_pair(own_half, arrived, bit_value == 1, axis_pos)
    kept_context = context_by_dest
    for bit_index in range(head_bit_flags):
        axis_pos = head_bit_flags - 1 - bit_index
        bit_value = device_number >> bit_index & 1
        own_half = lax.dynamic_index_in_dim(kept_context, bit_value, axis_pos, keepdims=False)
        sent_half = lax.dynamic_index_in_dim(kept_context, 1 - bit_value, axis_pos, keepdims=False)
        arrived = from_partner(sent_half, "tensor", bit_index)
        kept_context = stack_pair(own_half, arrived, bit_value == 1, axis_pos)
    cached_heads = kept_pairs.reshape(KEY_VALUE_HEADS, token_per_device, 2 * HEAD_SIZE)
    key_cache = cached_heads[:, :, :HEAD_SIZE][None]
    value_cache = cached_heads[:, :, HEAD_SIZE:][None]
    context_local = (
        kept_context.reshape(KEY_VALUE_HEADS, token_per_device, group_queries * HEAD_SIZE)
        .transpose(1, 0, 2)
        .reshape(token_per_device, QUERY_HEADS * HEAD_SIZE)
    )
    context_back = from_partner(context_local, "dp", 0)
    context = jnp.where(stay_here, context_local, context_back)[None]
    return (context, key_cache, value_cache)


def solution(mesh):
    placed = (P("dp", "tensor", None), P(), P("dp", "tensor"), P("tensor", None), P("tensor", None))
    return jax.shard_map(
        body,
        mesh=mesh,
        in_specs=placed,
        out_specs=(
            P("dp", "tensor", None),
            P("dp", None, "tensor", None),
            P("dp", None, "tensor", None),
        ),
        check_vma=False,
    )
```

```python
import jax
import jax.numpy as jnp
from jax import lax
from jax.experimental import pallas as pl
from jax.experimental.pallas import tpu as pltpu
from jax.sharding import PartitionSpec as P

QUERY_HEADS = 32
KEY_VALUE_HEADS = 8
HEAD_SIZE = 128
NSEG = 8
WINDOW = 512
SINKS = 4


rope_base = 500000.0
norm_eps = 1e-05


def rotary(values, angles):
    half_width = values.shape[-1] // 2
    first_half = values[..., :half_width]
    second_half = values[..., half_width:]
    cosine = jnp.cos(angles)
    sine_part = jnp.sin(angles)
    return jnp.concatenate(
        (
            first_half * cosine - second_half * sine_part,
            second_half * cosine + first_half * sine_part,
        ),
        -1,
    )


def gather_kernel(page, slab, note, pages, weights, notes, send, recv, local):
    dp = lax.axis_index("dp")
    t = lax.axis_index("tensor")
    core, zh = t % 2, (t // 2) % 4
    y, x = (t // 8) % 4, t // 32
    z = zh * 2 + dp
    q = t % 8

    def device(dx, dy, z_at, core_at):
        z_at = z_at % 8
        block = ((x + dx) % 4) * 4 + (y + dy) % 4
        return (z_at % 2, (block * 4 + z_at // 2) * 2 + core_at)

    slots = {}

    def copy(key, src, dst, target):
        i = slots.setdefault(key, len(slots))
        return pltpu.make_async_remote_copy(
            src_ref=src,
            dst_ref=dst,
            send_sem=send.at[i],
            recv_sem=recv.at[i],
            device_id=target,
            device_id_type=pl.DeviceIdType.MESH,
        )

    started = []

    def start(key, src, dst, target):
        c = copy(key, src, dst, target)
        c.start()
        started.append(c)

    partner = (dp, t + 1 - 2 * core)

    def arrived(key, dst):
        copy(key, dst, dst, partner).wait_recv()

    group = [(dp, (t // 8) * 8 + (q + r) % 8) for r in range(1, 8)]
    columns = [device(r, 0, z, core) for r in range(1, 4)]
    lines = [device(0, r, z, core) for r in range(1, 4)]
    ring = {1: device(0, 0, z + 1, core), -1: device(0, 0, z + 7, core)}
    barrier = pltpu.get_barrier_semaphore()
    peers = group + columns + lines + [ring[1], ring[-1]]
    for peer in peers:
        pl.semaphore_signal(barrier, inc=1, device_id=peer, device_id_type=pl.DeviceIdType.MESH)
    pl.semaphore_wait(barrier, len(peers))

    def page_at(dz, h, c):
        return pages.at[(z + dz + 8) % 8, c, h]

    def origin(order, da, db):
        dx, dy = (da, db) if order == 0 else (db, da)
        return weights.at[((x + dx + 4) % 4) * 4 + (y + dy + 4) % 4, order]

    def towards(order, da, db):
        dx, dy = (da, db) if order == 0 else (db, da)
        return device(dx + 4, dy + 4, z, core)

    own_copies = [
        pltpu.make_async_copy(page, pages.at[z, core], local.at[0]),
        pltpu.make_async_copy(slab, weights.at[x * 4 + y], local.at[1]),
        pltpu.make_async_copy(note, notes.at[y, x, q], local.at[2]),
    ]
    for c in own_copies:
        c.start()
    for r in range(1, 8):
        start(("note", r), note, notes.at[y, x, q], group[r - 1])
    for order in range(2):
        for d in (1, -1):
            start(("w1", order, d), slab.at[order], origin(order, 0, 0), towards(order, d, 0))
    for h in range(2):
        for d in (1, -1):
            start(("z", d, 0, h), page.at[h], page_at(0, h, core), ring[d])
    for order in range(2):
        for d in (1, -1):
            start(("w2", order, 0, d), slab.at[order], origin(order, 0, 0), towards(order, 0, d))
    for h in range(2):
        start(("c", 0, 0, h), page.at[h], page_at(0, h, core), partner)

    def page_step(s, h):
        for d in (1, -1):
            if s == 3 and h != (0 if d == 1 else 1):
                continue
            at = page_at(-d * (s + 1), h, core)
            arrived(("z", d, s, h), at)
            if s + 1 < 3 or (s + 1 == 3 and h == (0 if d == 1 else 1)):
                start(("z", d, s + 1, h), at, at, ring[d])
            start(("c", d, s, h), at, at, partner)

    def second_send(order, k):
        for d in (1, -1):
            start(("w2", order, k, d), origin(order, k, 0), origin(order, k, 0), towards(order, 0, d))

    def second_relay(order, k):
        for d in (1, -1):
            at = origin(order, k, -d)
            arrived(("w2", order, k, d), at)
            half = at.at[0 if d == 1 else 1]
            start(("w2r", order, k, d), half, half, towards(order, 0, d))

    for r in range(1, 8):
        arrived(("note", r), notes.at[y, x, (q + 8 - r) % 8])
    own_copies[2].wait()
    for r in range(1, 4):
        start(("notex", r), notes.at[y, x], notes.at[y, x], columns[r - 1])
    for order in range(2):
        for d in (1, -1):
            at = origin(order, -d, 0)
            arrived(("w1", order, d), at)
            half = at.at[0 if d == 1 else 1]
            start(("w1r", order, d), half, half, towards(order, d, 0))
            second_send(order, -d)
    for order in range(2):
        second_relay(order, 0)
    for r in range(1, 4):
        arrived(("notex", r), notes.at[y, (x + 4 - r) % 4])
    for r in range(1, 4):
        start(("notey", r), notes.at[y], notes.at[y], lines[r - 1])
    page_step(0, 0)
    for order in range(2):
        for d in (1, -1):
            arrived(("w1r", order, d), origin(order, -2 * d, 0).at[0 if d == 1 else 1])
        second_send(order, 2)
    for order in range(2):
        second_relay(order, -1)
        second_relay(order, 1)
    page_step(0, 1)
    for order in range(2):
        second_relay(order, 2)
    page_step(1, 0)
    for r in range(1, 4):
        arrived(("notey", r), notes.at[(y + 4 - r) % 4])
    for order in range(2):
        for k in (0, -1, 1, 2):
            for d in (1, -1):
                arrived(("w2r", order, k, d), origin(order, k, -2 * d).at[0 if d == 1 else 1])
    page_step(1, 1)
    for s, h in ((2, 0), (2, 1), (3, 0), (3, 1)):
        page_step(s, h)
    for h in range(2):
        arrived(("c", 0, 0, h), page_at(0, h, 1 - core))
    for s in range(4):
        for h in range(2):
            for d in (1, -1):
                if s < 3 or h == (0 if d == 1 else 1):
                    arrived(("c", d, s, h), page_at(-d * (s + 1), h, 1 - core))
    for c in started:
        c.wait_send()
    own_copies[0].wait()
    own_copies[1].wait()


COPIES = 7 + 3 + 3 + 14 + 16 + 4 + 4 + 16 + 16


def gather(page, slab, note):
    rows, width = page.shape
    depth, columns = slab.shape
    vmem = pl.BlockSpec(memory_space=pltpu.VMEM)
    hbm = pl.BlockSpec(memory_space=pltpu.HBM)
    return pl.pallas_call(
        gather_kernel,
        out_shape=(
            jax.ShapeDtypeStruct((8, 2, 2, rows // 2, width), page.dtype),
            jax.ShapeDtypeStruct((16, 2, 2, depth // 4, columns), slab.dtype),
            jax.ShapeDtypeStruct((4, 4, 8, 1, note.shape[0]), note.dtype),
        ),
        in_specs=[vmem] * 3,
        out_specs=(hbm,) * 3,
        scratch_shapes=[
            pltpu.SemaphoreType.DMA((COPIES,)),
            pltpu.SemaphoreType.DMA((COPIES,)),
            pltpu.SemaphoreType.DMA((3,)),
        ],
        compiler_params=pltpu.CompilerParams(collective_id=0, has_side_effects=True),
        name="gather",
    )(
        page.reshape(2, rows // 2, width),
        slab.reshape(2, 2, depth // 4, columns),
        note.reshape(1, -1),
    )


PAGE_ROWS = 128
REACH = WINDOW + PAGE_ROWS
CONTEXT_COPIES = 16
ATTEND_COPIES = CONTEXT_COPIES + 14 + 2 + 15


def attend_kernel(
    queries,
    keys,
    values,
    starts,
    sink_rows,
    sink_pairs,
    context,
    key_out,
    value_out,
    key_window,
    value_window,
    sinks,
    mixed,
    send,
    recv,
    local,
):
    dp = lax.axis_index("dp")
    t = lax.axis_index("tensor")
    core, zh = t % 2, (t // 2) % 4
    q, block = t % 8, t // 8
    width = mixed.shape[2]

    def copy(i, src, dst, target):
        return pltpu.make_async_remote_copy(
            src_ref=src,
            dst_ref=dst,
            send_sem=send.at[i],
            recv_sem=recv.at[i],
            device_id=target,
            device_id_type=pl.DeviceIdType.MESH,
        )

    def head(r):
        return (dp, block * 8 + (q + r) % 8)

    def plane(r):
        return (dp, ((block + r) % 16) * 8 + q)

    peers = [head(r) for r in range(1, 8)] + [plane(r) for r in range(1, 16)]
    peers += [(1 - dp, block * 8 + (q + r) % 8) for r in range(8)]
    barrier = pltpu.get_barrier_semaphore()
    for peer in peers:
        pl.semaphore_signal(barrier, inc=1, device_id=peer, device_id_type=pl.DeviceIdType.MESH)
    pl.semaphore_wait(barrier, len(peers))

    own_rows = pl.ds(WINDOW, keys.shape[0])
    last_rows = pl.ds(keys.shape[0] - WINDOW, WINDOW)
    first_rows = pl.ds(0, WINDOW)

    def page_rows(page):
        return pl.ds(pl.multiple_of(page * PAGE_ROWS, PAGE_ROWS), PAGE_ROWS)

    at = CONTEXT_COPIES
    sent = []
    for i, (source, target) in enumerate(((keys, key_window), (values, value_window))):
        c = copy(at + i, source.at[last_rows], target.at[first_rows], plane(1))
        c.start()
        sent.append(c)
    at += 2
    for r in range(1, 16):
        c = copy(at + r - 1, sink_pairs, sinks.at[block], plane(r))
        c.start()
        sent.append(c)
    locals_now = [
        pltpu.make_async_copy(keys, key_window.at[own_rows], local.at[0]),
        pltpu.make_async_copy(values, value_window.at[own_rows], local.at[1]),
        pltpu.make_async_copy(sink_pairs, sinks.at[block], local.at[2]),
        pltpu.make_async_copy(keys.at[page_rows(q)], key_out.at[q], local.at[3]),
        pltpu.make_async_copy(values.at[page_rows(q)], value_out.at[q], local.at[4]),
    ]
    for c in locals_now:
        c.start()
    at += 15
    for r in range(1, 8):
        page = (q + r) % 8
        for i, (source, target) in enumerate(((keys, key_out), (values, value_out))):
            c = copy(at + (r - 1) * 2 + i, source.at[page_rows(page)], target.at[q], head(r))
            c.start()
            sent.append(c)
    at = CONTEXT_COPIES
    for i, target in enumerate((key_window, value_window)):
        copy(at + i, target.at[first_rows], target.at[first_rows], plane(1)).wait_recv()
    at += 2
    for r in range(1, 16):
        landed = sinks.at[(block + 16 - r) % 16]
        copy(at + r - 1, landed, landed, plane(1)).wait_recv()
    for c in locals_now[:3]:
        c.wait()

    sink_sum = jnp.sum(sinks[...].astype(jnp.float32), 0).astype(jnp.bfloat16)
    sink_keys, sink_values = sink_sum[0], sink_sum[1]
    scale = HEAD_SIZE ** (-0.5)
    last_dims = (((1,), (1,)), ((), ()))

    def page_of(step):
        return ((zh + 3 - step // 2) % 4) * 2 + (core + 1 + step) % 2

    def columns(head_index):
        return pl.ds(pl.multiple_of(head_index * width, width), width)

    def to_half(step, half):
        target = context.at[dp, :, columns(q)]
        i = step if half == 0 else 8 + step
        side = dp if half == 0 else 1 - dp
        return copy(i, mixed.at[step], target, (side, block * 8 + page_of(step)))

    def attend(step, carry):
        page = page_of(step)
        rows = page_rows(page)
        row_start = starts[rows, :]
        first = block * keys.shape[0] + page * PAGE_ROWS
        query_pos = first + lax.broadcasted_iota(jnp.int32, (PAGE_ROWS, 1), 0)
        key_pos = first - WINDOW + lax.broadcasted_iota(jnp.int32, (PAGE_ROWS, REACH), 1)
        allowed = (
            (key_pos <= query_pos) & (key_pos >= row_start) & (key_pos >= query_pos - WINDOW)
        )
        sink_pos = sink_rows[0:1, :]
        sink_allowed = (
            (sink_rows[1:2, :] == row_start)
            & (sink_pos <= query_pos)
            & (sink_pos < query_pos - WINDOW)
        )
        reach = pl.ds(pl.multiple_of(page * PAGE_ROWS, PAGE_ROWS), REACH)
        near_keys = key_window[reach, :]
        near_values = value_window[reach, :]
        for h in range(width // HEAD_SIZE):
            part = pl.ds(h * HEAD_SIZE, HEAD_SIZE)
            query = queries[rows, part]
            scores = (
                lax.dot_general(query, near_keys, last_dims, preferred_element_type=jnp.float32)
                * scale
            )
            sink_scores = (
                lax.dot_general(query, sink_keys, last_dims, preferred_element_type=jnp.float32)
                * scale
            )
            scores = jnp.where(allowed, scores, -jnp.inf)
            sink_scores = jnp.where(sink_allowed, sink_scores, -jnp.inf)
            top = jnp.maximum(
                jnp.max(scores, -1, keepdims=True), jnp.max(sink_scores, -1, keepdims=True)
            )
            near = jnp.exp(scores - top)
            far = jnp.exp(sink_scores - top)
            inverse = 1.0 / (
                jnp.sum(near, -1, keepdims=True) + jnp.sum(far, -1, keepdims=True)
            )
            result = jnp.dot(
                (near * inverse).astype(jnp.bfloat16),
                near_values,
                preferred_element_type=jnp.float32,
            ) + jnp.dot(
                (far * inverse).astype(jnp.bfloat16),
                sink_values,
                preferred_element_type=jnp.float32,
            )
            mixed[step, :, part] = result.astype(jnp.bfloat16)

        @pl.when(step > 0)
        def _():
            for half in range(2):
                to_half(step - 1, half).start()

        return carry

    lax.fori_loop(0, 8, attend, 0)
    at = CONTEXT_COPIES + 2 + 15
    for r in range(1, 8):
        for i, target in enumerate((key_out, value_out)):
            landed = target.at[(q + 8 - r) % 8]
            copy(at + (r - 1) * 2 + i, landed, landed, head(1)).wait_recv()
    for c in sent:
        c.wait_send()
    for c in locals_now[3:]:
        c.wait()
    own = pltpu.make_async_copy(mixed.at[7], context.at[dp, :, columns(q)], local.at[5])
    own.start()
    to_half(7, 1).start()
    for step in range(8):
        source = ((zh + 4 - 3 + step // 2) % 4) * 2 + (core + 1 + step) % 2
        for i, half in enumerate((dp, 1 - dp)):
            if i == 0 and step == 7:
                continue
            landed = context.at[half, :, columns(source)]
            copy(i * 8 + step, landed, landed, head(1)).wait_recv()
    for step in range(8):
        if step < 7:
            to_half(step, 0).wait_send()
        to_half(step, 1).wait_send()
    own.wait()


def attend_pages(queries, keys, values, starts, sink_rows, sink_pairs):
    rows, width = queries.shape
    vmem = pl.BlockSpec(memory_space=pltpu.VMEM)
    hbm = pl.BlockSpec(memory_space=pltpu.HBM)
    cache = jax.ShapeDtypeStruct((KEY_VALUE_HEADS, PAGE_ROWS, HEAD_SIZE), keys.dtype)
    return pl.pallas_call(
        attend_kernel,
        out_shape=(
            jax.ShapeDtypeStruct((2, PAGE_ROWS, KEY_VALUE_HEADS * width), queries.dtype),
            cache,
            cache,
        ),
        in_specs=[vmem] * 6,
        out_specs=(hbm,) * 3,
        scratch_shapes=[
            pltpu.VMEM((WINDOW + rows, HEAD_SIZE), keys.dtype),
            pltpu.VMEM((WINDOW + rows, HEAD_SIZE), keys.dtype),
            pltpu.VMEM((16,) + sink_pairs.shape, sink_pairs.dtype),
            pltpu.VMEM((8, PAGE_ROWS, width), queries.dtype),
            pltpu.SemaphoreType.DMA((ATTEND_COPIES,)),
            pltpu.SemaphoreType.DMA((ATTEND_COPIES,)),
            pltpu.SemaphoreType.DMA((6,)),
        ],
        compiler_params=pltpu.CompilerParams(collective_id=1, has_side_effects=True),
        name="attend",
    )(queries, keys, values, starts, sink_rows, sink_pairs)


def body(tokens, norm_gain, segments, deal_table, projection):
    group_id = lax.axis_index("dp")
    device_number = lax.axis_index("tensor")
    token_per_device = tokens.shape[1]
    model_width = tokens.shape[2]
    block_length = KEY_VALUE_HEADS * token_per_device
    block_number = device_number // KEY_VALUE_HEADS
    group_queries = QUERY_HEADS // KEY_VALUE_HEADS
    own_page = tokens[0]
    owner_group = jnp.sum(jnp.where(jnp.arange(deal_table.shape[1]) == group_id, deal_table[0], 0))
    stay_here = owner_group == group_id
    widened = own_page.astype(jnp.float32)
    normed = (
        widened * lax.rsqrt(jnp.mean(widened * widened, -1, keepdims=True) + norm_eps) * norm_gain
    ).astype(jnp.bfloat16)
    client = jnp.where(stay_here, group_id, 1 - group_id).astype(jnp.int32)
    note = jnp.concatenate((segments[0], jnp.broadcast_to(client, segments[0].shape)))
    pages, weights, notes = gather(normed, projection, note)
    weights_held = weights.reshape(model_width, projection.shape[1])
    notes = notes.reshape(4, 4, KEY_VALUE_HEADS, 2, token_per_device).transpose(1, 0, 2, 3, 4)
    notes = notes.reshape(-1, KEY_VALUE_HEADS, 2, token_per_device)
    counts_int = jnp.sum(
        (notes[:, :, 0, :, None] == jnp.arange(NSEG)).astype(jnp.int32), (0, 1, 2)
    )
    seg_starts = jnp.cumsum(counts_int) - counts_int
    own_notes = lax.dynamic_index_in_dim(notes, block_number, 0, keepdims=False)
    segment_match = own_notes[:, 0].reshape(block_length)[:, None] == jnp.arange(NSEG)[None, :]
    starts_block = jnp.sum(jnp.where(segment_match, seg_starts[None, :], 0), 1)
    clients = own_notes[:, 1, 0].reshape(4, 2, 1, 1)
    pages = pages.reshape(4, 2, 2, token_per_device, model_width)
    rows_block = jnp.where(clients == 1, pages[:, 1], pages[:, 0]).reshape(
        block_length, model_width
    )
    projected = jnp.dot(rows_block, weights_held, preferred_element_type=jnp.float32)
    rope_freq = rope_base ** (-(jnp.arange(0, HEAD_SIZE, 2).astype(jnp.float32) / HEAD_SIZE))
    block_positions = block_number * block_length + jnp.arange(block_length)
    angles = (block_positions - starts_block).astype(jnp.float32)[:, None] * rope_freq[None, :]
    queries = rotary(
        projected[:, : group_queries * HEAD_SIZE].reshape(block_length, group_queries, HEAD_SIZE),
        angles[:, None, :],
    ).astype(jnp.bfloat16)
    keys_own = rotary(
        projected[:, group_queries * HEAD_SIZE : (group_queries + 1) * HEAD_SIZE], angles
    ).astype(jnp.bfloat16)
    values_own = projected[:, (group_queries + 1) * HEAD_SIZE :].astype(jnp.bfloat16)
    local_pairs = jnp.stack((keys_own, values_own))
    sink_positions = (seg_starts[:, None] + jnp.arange(SINKS)[None, :]).reshape(NSEG * SINKS)
    local_rows = sink_positions - block_number * block_length
    selector = (local_rows[:, None] == jnp.arange(block_length)[None, :]).astype(jnp.bfloat16)
    sink_pairs = jnp.einsum(
        "sr,prd->psd", selector, local_pairs, preferred_element_type=jnp.float32
    ).astype(jnp.bfloat16)
    sink_rows = jnp.stack((sink_positions, jnp.repeat(seg_starts, SINKS)))
    contexts, key_cache, value_cache = attend_pages(
        queries.reshape(block_length, group_queries * HEAD_SIZE),
        keys_own,
        values_own,
        starts_block[:, None],
        sink_rows,
        sink_pairs,
    )
    context = jnp.where(owner_group == 1, contexts[1], contexts[0])
    return (context[None], key_cache[None], value_cache[None])


def solution(mesh):
    placed = (P("dp", "tensor", None), P(), P("dp", "tensor"), P("tensor", None), P("tensor", None))
    return jax.shard_map(
        body,
        mesh=mesh,
        in_specs=placed,
        out_specs=(
            P("dp", "tensor", None),
            P("dp", None, "tensor", None),
            P("dp", None, "tensor", None),
        ),
        check_vma=False,
    )
```

```python
import jax
import jax.numpy as jnp
from jax import lax
from jax.experimental import pallas as pl
from jax.experimental.pallas import tpu as pltpu
from jax.sharding import PartitionSpec as P

QUERY_HEADS = 32
KEY_VALUE_HEADS = 8
HEAD_SIZE = 128
NSEG = 8
WINDOW = 512
SINKS = 4


rope_base = 500000.0
norm_eps = 1e-05


def rotary(values, angles):
    half_width = values.shape[-1] // 2
    first_half = values[..., :half_width]
    second_half = values[..., half_width:]
    cosine = jnp.cos(angles)
    sine_part = jnp.sin(angles)
    return jnp.concatenate(
        (
            first_half * cosine - second_half * sine_part,
            second_half * cosine + first_half * sine_part,
        ),
        -1,
    )


def gather_kernel(page, slab, note, pages, weights, notes, send, recv, local):
    dp = lax.axis_index("dp")
    t = lax.axis_index("tensor")
    core, zh = t % 2, (t // 2) % 4
    y, x = (t // 8) % 4, t // 32
    z = zh * 2 + dp
    q = t % 8

    def device(dx, dy, z_at, core_at):
        z_at = z_at % 8
        block = ((x + dx) % 4) * 4 + (y + dy) % 4
        return (z_at % 2, (block * 4 + z_at // 2) * 2 + core_at)

    slots = {}

    def copy(key, src, dst, target):
        i = slots.setdefault(key, len(slots))
        return pltpu.make_async_remote_copy(
            src_ref=src,
            dst_ref=dst,
            send_sem=send.at[i],
            recv_sem=recv.at[i],
            device_id=target,
            device_id_type=pl.DeviceIdType.MESH,
        )

    started = []

    def start(key, src, dst, target):
        c = copy(key, src, dst, target)
        c.start()
        started.append(c)

    partner = (dp, t + 1 - 2 * core)

    def arrived(key, dst):
        copy(key, dst, dst, partner).wait_recv()

    group = [(dp, (t // 8) * 8 + (q + r) % 8) for r in range(1, 8)]
    columns = [device(r, 0, z, core) for r in range(1, 4)]
    lines = [device(0, r, z, core) for r in range(1, 4)]
    ring = {1: device(0, 0, z + 1, core), -1: device(0, 0, z + 7, core)}
    barrier = pltpu.get_barrier_semaphore()
    peers = group + columns + lines + [ring[1], ring[-1]]
    for peer in peers:
        pl.semaphore_signal(barrier, inc=1, device_id=peer, device_id_type=pl.DeviceIdType.MESH)
    pl.semaphore_wait(barrier, len(peers))

    def page_at(dz, h, c):
        return pages.at[(z + dz + 8) % 8, c, h]

    def origin(order, da, db):
        dx, dy = (da, db) if order == 0 else (db, da)
        return weights.at[((x + dx + 4) % 4) * 4 + (y + dy + 4) % 4, order]

    def towards(order, da, db):
        dx, dy = (da, db) if order == 0 else (db, da)
        return device(dx + 4, dy + 4, z, core)

    own_copies = [
        pltpu.make_async_copy(page, pages.at[z, core], local.at[0]),
        pltpu.make_async_copy(slab, weights.at[x * 4 + y], local.at[1]),
        pltpu.make_async_copy(note, notes.at[y, x, q], local.at[2]),
    ]
    for c in own_copies:
        c.start()
    for r in range(1, 8):
        start(("note", r), note, notes.at[y, x, q], group[r - 1])
    for order in range(2):
        for d in (1, -1):
            start(("w1", order, d), slab.at[order], origin(order, 0, 0), towards(order, d, 0))
    for h in range(2):
        for d in (1, -1):
            start(("z", d, 0, h), page.at[h], page_at(0, h, core), ring[d])
    for order in range(2):
        for d in (1, -1):
            start(("w2", order, 0, d), slab.at[order], origin(order, 0, 0), towards(order, 0, d))
    for h in range(2):
        start(("c", 0, 0, h), page.at[h], page_at(0, h, core), partner)

    def page_step(s, h):
        for d in (1, -1):
            if s == 3 and h != (0 if d == 1 else 1):
                continue
            at = page_at(-d * (s + 1), h, core)
            arrived(("z", d, s, h), at)
            if s + 1 < 3 or (s + 1 == 3 and h == (0 if d == 1 else 1)):
                start(("z", d, s + 1, h), at, at, ring[d])
            start(("c", d, s, h), at, at, partner)

    def second_send(order, k):
        for d in (1, -1):
            start(("w2", order, k, d), origin(order, k, 0), origin(order, k, 0), towards(order, 0, d))

    def second_relay(order, k):
        for d in (1, -1):
            at = origin(order, k, -d)
            arrived(("w2", order, k, d), at)
            half = at.at[0 if d == 1 else 1]
            start(("w2r", order, k, d), half, half, towards(order, 0, d))

    for r in range(1, 8):
        arrived(("note", r), notes.at[y, x, (q + 8 - r) % 8])
    own_copies[2].wait()
    for r in range(1, 4):
        start(("notex", r), notes.at[y, x], notes.at[y, x], columns[r - 1])
    for order in range(2):
        for d in (1, -1):
            at = origin(order, -d, 0)
            arrived(("w1", order, d), at)
            half = at.at[0 if d == 1 else 1]
            start(("w1r", order, d), half, half, towards(order, d, 0))
            second_send(order, -d)
    for order in range(2):
        second_relay(order, 0)
    for r in range(1, 4):
        arrived(("notex", r), notes.at[y, (x + 4 - r) % 4])
    for r in range(1, 4):
        start(("notey", r), notes.at[y], notes.at[y], lines[r - 1])
    page_step(0, 0)
    for order in range(2):
        for d in (1, -1):
            arrived(("w1r", order, d), origin(order, -2 * d, 0).at[0 if d == 1 else 1])
        second_send(order, 2)
    for order in range(2):
        second_relay(order, -1)
        second_relay(order, 1)
    page_step(0, 1)
    for order in range(2):
        second_relay(order, 2)
    page_step(1, 0)
    for r in range(1, 4):
        arrived(("notey", r), notes.at[(y + 4 - r) % 4])
    for order in range(2):
        for k in (0, -1, 1, 2):
            for d in (1, -1):
                arrived(("w2r", order, k, d), origin(order, k, -2 * d).at[0 if d == 1 else 1])
    page_step(1, 1)
    for s, h in ((2, 0), (2, 1), (3, 0), (3, 1)):
        page_step(s, h)
    for h in range(2):
        arrived(("c", 0, 0, h), page_at(0, h, 1 - core))
    for s in range(4):
        for h in range(2):
            for d in (1, -1):
                if s < 3 or h == (0 if d == 1 else 1):
                    arrived(("c", d, s, h), page_at(-d * (s + 1), h, 1 - core))
    for c in started:
        c.wait_send()
    own_copies[0].wait()
    own_copies[1].wait()


COPIES = 7 + 3 + 3 + 14 + 16 + 4 + 4 + 16 + 16


def gather(page, slab, note):
    rows, width = page.shape
    depth, columns = slab.shape
    vmem = pl.BlockSpec(memory_space=pltpu.VMEM)
    hbm = pl.BlockSpec(memory_space=pltpu.HBM)
    return pl.pallas_call(
        gather_kernel,
        out_shape=(
            jax.ShapeDtypeStruct((8, 2, 2, rows // 2, width), page.dtype),
            jax.ShapeDtypeStruct((16, 2, 2, depth // 4, columns), slab.dtype),
            jax.ShapeDtypeStruct((4, 4, 8, 1, note.shape[0]), note.dtype),
        ),
        in_specs=[vmem] * 3,
        out_specs=(hbm,) * 3,
        scratch_shapes=[
            pltpu.SemaphoreType.DMA((COPIES,)),
            pltpu.SemaphoreType.DMA((COPIES,)),
            pltpu.SemaphoreType.DMA((3,)),
        ],
        compiler_params=pltpu.CompilerParams(collective_id=0, has_side_effects=True),
        name="gather",
    )(
        page.reshape(2, rows // 2, width),
        slab.reshape(2, 2, depth // 4, columns),
        note.reshape(1, -1),
    )


PAGE_ROWS = 128
REACH = WINDOW + PAGE_ROWS
CONTEXT_COPIES = 16
ATTEND_COPIES = CONTEXT_COPIES + 2 + 15 + 16 + 4
FAR = 2


def attend_kernel(
    queries,
    keys,
    values,
    starts,
    sink_rows,
    sink_pairs,
    context,
    key_out,
    value_out,
    key_window,
    value_window,
    sinks,
    mixed,
    passing,
    send,
    recv,
    local,
):
    dp = lax.axis_index("dp")
    t = lax.axis_index("tensor")
    core, zh = t % 2, (t // 2) % 4
    q, block = t % 8, t // 8
    width = mixed.shape[2]

    def copy(i, src, dst, target):
        return pltpu.make_async_remote_copy(
            src_ref=src,
            dst_ref=dst,
            send_sem=send.at[i],
            recv_sem=recv.at[i],
            device_id=target,
            device_id_type=pl.DeviceIdType.MESH,
        )

    def head(r):
        return (dp, block * 8 + (q + r) % 8)

    def page_near(shift, flip):
        return ((zh + shift) % 4) * 2 + (core + flip) % 2

    partner = (1 - dp, t)

    def plane(r):
        return (dp, ((block + r) % 16) * 8 + q)

    peers = [head(r) for r in range(1, 8)] + [plane(r) for r in range(1, 16)]
    peers += [(1 - dp, block * 8 + (q + r) % 8) for r in range(8)]
    barrier = pltpu.get_barrier_semaphore()
    for peer in peers:
        pl.semaphore_signal(barrier, inc=1, device_id=peer, device_id_type=pl.DeviceIdType.MESH)
    pl.semaphore_wait(barrier, len(peers))

    own_rows = pl.ds(WINDOW, keys.shape[0])
    last_rows = pl.ds(keys.shape[0] - WINDOW, WINDOW)
    first_rows = pl.ds(0, WINDOW)

    def page_rows(page):
        return pl.ds(pl.multiple_of(page * PAGE_ROWS, PAGE_ROWS), PAGE_ROWS)

    at = CONTEXT_COPIES
    sent = []
    for i, (source, target) in enumerate(((keys, key_window), (values, value_window))):
        c = copy(at + i, source.at[last_rows], target.at[first_rows], plane(1))
        c.start()
        sent.append(c)
    at += 2
    for r in range(1, 16):
        c = copy(at + r - 1, sink_pairs, sinks.at[block], plane(r))
        c.start()
        sent.append(c)
    locals_now = [
        pltpu.make_async_copy(keys, key_window.at[own_rows], local.at[0]),
        pltpu.make_async_copy(values, value_window.at[own_rows], local.at[1]),
        pltpu.make_async_copy(sink_pairs, sinks.at[block], local.at[2]),
        pltpu.make_async_copy(keys.at[page_rows(q)], key_out.at[q], local.at[3]),
        pltpu.make_async_copy(values.at[page_rows(q)], value_out.at[q], local.at[4]),
    ]
    for c in locals_now:
        c.start()
    caches = ((keys, key_out), (values, value_out))
    spread = [(shift, flip) for shift in (FAR, 3, 1, 0) for flip in (1, 0)][:7]

    def cache_slot(shift, flip, i):
        return CONTEXT_COPIES + 17 + (shift * 2 + flip) * 2 + i

    def passing_slot(flip, i):
        return CONTEXT_COPIES + 33 + flip * 2 + i

    for shift, flip in spread:
        page = page_near(shift, flip)
        for i, (source, target) in enumerate(caches):
            piece = source.at[page_rows(page)]
            if shift == FAR:
                c = copy(
                    passing_slot(flip, i), piece, passing.at[i, flip], (1 - dp, block * 8 + page)
                )
            else:
                c = copy(cache_slot(shift, flip, i), piece, target.at[q], (dp, block * 8 + page))
            c.start()
            sent.append(c)

    def hand_on(flip, i):
        piece = passing.at[i, flip]
        source = page_near(4 - FAR, flip)
        return copy(cache_slot(FAR, flip, i), piece, caches[i][1].at[source], partner)

    at = CONTEXT_COPIES
    for i, target in enumerate((key_window, value_window)):
        copy(at + i, target.at[first_rows], target.at[first_rows], plane(1)).wait_recv()
    at += 2
    for r in range(1, 16):
        landed = sinks.at[(block + 16 - r) % 16]
        copy(at + r - 1, landed, landed, plane(1)).wait_recv()
    for c in locals_now[:3]:
        c.wait()

    sink_sum = jnp.sum(sinks[...].astype(jnp.float32), 0).astype(jnp.bfloat16)
    sink_keys, sink_values = sink_sum[0], sink_sum[1]
    scale = HEAD_SIZE ** (-0.5)
    last_dims = (((1,), (1,)), ((), ()))

    def page_of(step):
        turn = step // 2
        return page_near(FAR + turn * (turn + 1) // 2, 1 + step)

    def columns(head_index):
        return pl.ds(pl.multiple_of(head_index * width, width), width)

    def to_half(step, half):
        target = context.at[dp, :, columns(q)]
        i = step if half == 0 else 8 + step
        side = dp if half == 0 else 1 - dp
        return copy(i, mixed.at[step], target, (side, block * 8 + page_of(step)))

    def attend(step, carry):
        page = page_of(step)
        rows = page_rows(page)
        row_start = starts[rows, :]
        first = block * keys.shape[0] + page * PAGE_ROWS
        query_pos = first + lax.broadcasted_iota(jnp.int32, (PAGE_ROWS, 1), 0)
        key_pos = first - WINDOW + lax.broadcasted_iota(jnp.int32, (PAGE_ROWS, REACH), 1)
        allowed = (
            (key_pos <= query_pos) & (key_pos >= row_start) & (key_pos >= query_pos - WINDOW)
        )
        sink_pos = sink_rows[0:1, :]
        sink_allowed = (
            (sink_rows[1:2, :] == row_start)
            & (sink_pos <= query_pos)
            & (sink_pos < query_pos - WINDOW)
        )
        reach = pl.ds(pl.multiple_of(page * PAGE_ROWS, PAGE_ROWS), REACH)
        near_keys = key_window[reach, :]
        near_values = value_window[reach, :]
        for h in range(width // HEAD_SIZE):
            part = pl.ds(h * HEAD_SIZE, HEAD_SIZE)
            query = queries[rows, part]
            scores = (
                lax.dot_general(query, near_keys, last_dims, preferred_element_type=jnp.float32)
                * scale
            )
            sink_scores = (
                lax.dot_general(query, sink_keys, last_dims, preferred_element_type=jnp.float32)
                * scale
            )
            scores = jnp.where(allowed, scores, -jnp.inf)
            sink_scores = jnp.where(sink_allowed, sink_scores, -jnp.inf)
            top = jnp.maximum(
                jnp.max(scores, -1, keepdims=True), jnp.max(sink_scores, -1, keepdims=True)
            )
            near = jnp.exp(scores - top)
            far = jnp.exp(sink_scores - top)
            inverse = 1.0 / (
                jnp.sum(near, -1, keepdims=True) + jnp.sum(far, -1, keepdims=True)
            )
            result = jnp.dot(
                (near * inverse).astype(jnp.bfloat16),
                near_values,
                preferred_element_type=jnp.float32,
            ) + jnp.dot(
                (far * inverse).astype(jnp.bfloat16),
                sink_values,
                preferred_element_type=jnp.float32,
            )
            mixed[step, :, part] = result.astype(jnp.bfloat16)

        @pl.when(step > 0)
        def _():
            to_half(step - 1, 1).start()

        @pl.when(step > 2)
        def _():
            to_half(step - 1, 0).start()

        @pl.when(step == 2)
        def _():
            for flip in range(2):
                for i in range(2):
                    piece = passing.at[i, flip]
                    copy(passing_slot(flip, i), piece, piece, partner).wait_recv()
                    hand_on(flip, i).start()

        return carry

    lax.fori_loop(0, 8, attend, 0)
    own = pltpu.make_async_copy(mixed.at[7], context.at[dp, :, columns(q)], local.at[5])
    own.start()
    to_half(7, 1).start()

    def source_of(step):
        turn = step // 2
        return page_near(8 - FAR - turn * (turn + 1) // 2, 1 + step)

    def landed(step, half):
        return context.at[dp if half == 0 else 1 - dp, :, columns(source_of(step))]

    def pass_context(step):
        piece = landed(step, 1)
        return copy(step, piece, piece, partner)

    for step in range(2):
        copy(8 + step, landed(step, 1), landed(step, 1), partner).wait_recv()
        pass_context(step).start()
    for shift, flip in spread:
        source = page_near(4 - shift, flip)
        for i in range(2):
            piece = caches[i][1].at[source]
            copy(cache_slot(shift, flip, i), piece, piece, partner).wait_recv()
    for step in range(2, 8):
        copy(8 + step, landed(step, 1), landed(step, 1), partner).wait_recv()
    for step in range(7):
        copy(step, landed(step, 0), landed(step, 0), partner).wait_recv()
    for c in sent + [hand_on(flip, i) for flip in range(2) for i in range(2)]:
        c.wait_send()
    for c in locals_now[3:]:
        c.wait()
    for step in range(8):
        if step < 2:
            pass_context(step).wait_send()
        elif step < 7:
            to_half(step, 0).wait_send()
        to_half(step, 1).wait_send()
    own.wait()


def attend_pages(queries, keys, values, starts, sink_rows, sink_pairs):
    rows, width = queries.shape
    vmem = pl.BlockSpec(memory_space=pltpu.VMEM)
    hbm = pl.BlockSpec(memory_space=pltpu.HBM)
    cache = jax.ShapeDtypeStruct((KEY_VALUE_HEADS, PAGE_ROWS, HEAD_SIZE), keys.dtype)
    return pl.pallas_call(
        attend_kernel,
        out_shape=(
            jax.ShapeDtypeStruct((2, PAGE_ROWS, KEY_VALUE_HEADS * width), queries.dtype),
            cache,
            cache,
        ),
        in_specs=[vmem] * 6,
        out_specs=(hbm,) * 3,
        scratch_shapes=[
            pltpu.VMEM((WINDOW + rows, HEAD_SIZE), keys.dtype),
            pltpu.VMEM((WINDOW + rows, HEAD_SIZE), keys.dtype),
            pltpu.VMEM((16,) + sink_pairs.shape, sink_pairs.dtype),
            pltpu.VMEM((8, PAGE_ROWS, width), queries.dtype),
            pltpu.VMEM((2, 2, PAGE_ROWS, HEAD_SIZE), keys.dtype),
            pltpu.SemaphoreType.DMA((ATTEND_COPIES,)),
            pltpu.SemaphoreType.DMA((ATTEND_COPIES,)),
            pltpu.SemaphoreType.DMA((6,)),
        ],
        compiler_params=pltpu.CompilerParams(collective_id=1, has_side_effects=True),
        name="attend",
    )(queries, keys, values, starts, sink_rows, sink_pairs)


def body(tokens, norm_gain, segments, deal_table, projection):
    group_id = lax.axis_index("dp")
    device_number = lax.axis_index("tensor")
    token_per_device = tokens.shape[1]
    model_width = tokens.shape[2]
    block_length = KEY_VALUE_HEADS * token_per_device
    block_number = device_number // KEY_VALUE_HEADS
    group_queries = QUERY_HEADS // KEY_VALUE_HEADS
    own_page = tokens[0]
    owner_group = jnp.sum(jnp.where(jnp.arange(deal_table.shape[1]) == group_id, deal_table[0], 0))
    stay_here = owner_group == group_id
    widened = own_page.astype(jnp.float32)
    normed = (
        widened * lax.rsqrt(jnp.mean(widened * widened, -1, keepdims=True) + norm_eps) * norm_gain
    ).astype(jnp.bfloat16)
    client = jnp.where(stay_here, group_id, 1 - group_id).astype(jnp.int32)
    note = jnp.concatenate((segments[0], jnp.broadcast_to(client, segments[0].shape)))
    pages, weights, notes = gather(normed, projection, note)
    weights_held = weights.reshape(model_width, projection.shape[1])
    notes = notes.reshape(4, 4, KEY_VALUE_HEADS, 2, token_per_device).transpose(1, 0, 2, 3, 4)
    notes = notes.reshape(-1, KEY_VALUE_HEADS, 2, token_per_device)
    counts_int = jnp.sum(
        (notes[:, :, 0, :, None] == jnp.arange(NSEG)).astype(jnp.int32), (0, 1, 2)
    )
    seg_starts = jnp.cumsum(counts_int) - counts_int
    own_notes = lax.dynamic_index_in_dim(notes, block_number, 0, keepdims=False)
    segment_match = own_notes[:, 0].reshape(block_length)[:, None] == jnp.arange(NSEG)[None, :]
    starts_block = jnp.sum(jnp.where(segment_match, seg_starts[None, :], 0), 1)
    clients = own_notes[:, 1, 0].reshape(4, 2, 1, 1)
    pages = pages.reshape(4, 2, 2, token_per_device, model_width)
    rows_block = jnp.where(clients == 1, pages[:, 1], pages[:, 0]).reshape(
        block_length, model_width
    )
    projected = jnp.dot(rows_block, weights_held, preferred_element_type=jnp.float32)
    rope_freq = rope_base ** (-(jnp.arange(0, HEAD_SIZE, 2).astype(jnp.float32) / HEAD_SIZE))
    block_positions = block_number * block_length + jnp.arange(block_length)
    angles = (block_positions - starts_block).astype(jnp.float32)[:, None] * rope_freq[None, :]
    queries = rotary(
        projected[:, : group_queries * HEAD_SIZE].reshape(block_length, group_queries, HEAD_SIZE),
        angles[:, None, :],
    ).astype(jnp.bfloat16)
    keys_own = rotary(
        projected[:, group_queries * HEAD_SIZE : (group_queries + 1) * HEAD_SIZE], angles
    ).astype(jnp.bfloat16)
    values_own = projected[:, (group_queries + 1) * HEAD_SIZE :].astype(jnp.bfloat16)
    local_pairs = jnp.stack((keys_own, values_own))
    sink_positions = (seg_starts[:, None] + jnp.arange(SINKS)[None, :]).reshape(NSEG * SINKS)
    local_rows = sink_positions - block_number * block_length
    selector = (local_rows[:, None] == jnp.arange(block_length)[None, :]).astype(jnp.bfloat16)
    sink_pairs = jnp.einsum(
        "sr,prd->psd", selector, local_pairs, preferred_element_type=jnp.float32
    ).astype(jnp.bfloat16)
    sink_rows = jnp.stack((sink_positions, jnp.repeat(seg_starts, SINKS)))
    contexts, key_cache, value_cache = attend_pages(
        queries.reshape(block_length, group_queries * HEAD_SIZE),
        keys_own,
        values_own,
        starts_block[:, None],
        sink_rows,
        sink_pairs,
    )
    context = jnp.where(owner_group == 1, contexts[1], contexts[0])
    return (context[None], key_cache[None], value_cache[None])


def solution(mesh):
    placed = (P("dp", "tensor", None), P(), P("dp", "tensor"), P("tensor", None), P("tensor", None))
    return jax.shard_map(
        body,
        mesh=mesh,
        in_specs=placed,
        out_specs=(
            P("dp", "tensor", None),
            P("dp", None, "tensor", None),
            P("dp", None, "tensor", None),
        ),
        check_vma=False,
    )
```

```python
import jax
import jax.numpy as jnp
from jax import lax
from jax.experimental import pallas as pl
from jax.experimental.pallas import tpu as pltpu
from jax.sharding import PartitionSpec as P

QUERY_HEADS = 32
KEY_VALUE_HEADS = 8
HEAD_SIZE = 128
NSEG = 8
WINDOW = 512
SINKS = 4


rope_base = 500000.0
norm_eps = 1e-05


def gather_kernel(
    page,
    slab,
    note,
    gain,
    freq,
    queries,
    keys,
    values,
    starts,
    sink_rows,
    sink_pairs,
    pages,
    weights,
    notes,
    normed,
    send,
    recv,
    local,
):
    dp = lax.axis_index("dp")
    t = lax.axis_index("tensor")
    core, zh = t % 2, (t // 2) % 4
    y, x = (t // 8) % 4, t // 32
    z = zh * 2 + dp
    q = t % 8

    def device(dx, dy, z_at, core_at):
        z_at = z_at % 8
        block = ((x + dx) % 4) * 4 + (y + dy) % 4
        return (z_at % 2, (block * 4 + z_at // 2) * 2 + core_at)

    slots = {}

    def copy(key, src, dst, target):
        i = slots.setdefault(key, len(slots))
        return pltpu.make_async_remote_copy(
            src_ref=src,
            dst_ref=dst,
            send_sem=send.at[i],
            recv_sem=recv.at[i],
            device_id=target,
            device_id_type=pl.DeviceIdType.MESH,
        )

    started = []

    def start(key, src, dst, target):
        c = copy(key, src, dst, target)
        c.start()
        started.append(c)

    partner = (dp, t + 1 - 2 * core)

    def arrived(key, dst):
        copy(key, dst, dst, partner).wait_recv()

    group = [(dp, (t // 8) * 8 + (q + r) % 8) for r in range(1, 8)]
    columns = [device(r, 0, z, core) for r in range(1, 4)]
    lines = [device(0, r, z, core) for r in range(1, 4)]
    ring = {1: device(0, 0, z + 1, core), -1: device(0, 0, z + 7, core)}
    barrier = pltpu.get_barrier_semaphore()
    peers = group + columns + lines + [ring[1], ring[-1]]
    for peer in peers:
        pl.semaphore_signal(barrier, inc=1, device_id=peer, device_id_type=pl.DeviceIdType.MESH)
    pl.semaphore_wait(barrier, len(peers))

    def page_at(dz, h, c):
        return pages.at[(z + dz + 8) % 8, c, h]

    def origin(order, da, db):
        dx, dy = (da, db) if order == 0 else (db, da)
        return weights.at[((x + dx + 4) % 4) * 4 + (y + dy + 4) % 4, order]

    def towards(order, da, db):
        dx, dy = (da, db) if order == 0 else (db, da)
        return device(dx + 4, dy + 4, z, core)

    page_count = 2 * page.shape[1]
    pair_count = 2 * page_count
    model_width = page.shape[2]
    query_width = queries.shape[1]
    depth = 4 * slab.shape[2]
    per_step = model_width // 4
    block = x * 4 + y

    def seg_starts():
        ids = notes[:, :, :, :, 0:page_count]
        found = []
        for segment in range(NSEG):
            below = jnp.sum((ids < segment).astype(jnp.float32), (0, 1, 2))
            found.append(jnp.sum(below, -1, keepdims=True))
        return found

    def rotated(block_values, cosine, sine):
        half = HEAD_SIZE // 2
        first, second = block_values[:, :half], block_values[:, half:]
        return jnp.concatenate(
            (first * cosine - second * sine, second * cosine + first * sine), -1
        ).astype(jnp.bfloat16)

    def project(shift):
        pair = (zh + shift) % 4
        found = seg_starts()
        eye = lax.broadcasted_iota(jnp.int32, (page_count, page_count), 0)
        eye = eye == lax.broadcasted_iota(jnp.int32, (page_count, page_count), 1)
        columns = []
        for c in range(2):
            told = notes[y, x, pair * 2 + c]
            ids, client = told[:, :page_count], told[:, page_count:]
            start_row = jnp.zeros(ids.shape, jnp.float32)
            for segment in range(NSEG):
                start_row = jnp.where(ids == segment, found[segment], start_row)
            start_row = jnp.broadcast_to(start_row, (page_count, page_count))
            columns.append(jnp.sum(jnp.where(eye, start_row, 0.0), 1, keepdims=True))
            upper = jnp.tile(client, (1, model_width // page_count)) == 1
            upper = jnp.broadcast_to(upper, (16, model_width))
            for h in range(2):

                def norm(i, carry, c=c, h=h, upper=upper):
                    rows = pl.ds(pl.multiple_of(i * 16, 16), 16)
                    wide = jnp.where(
                        upper,
                        pages[pair * 2 + 1, c, h, rows, :].astype(jnp.float32),
                        pages[pair * 2, c, h, rows, :].astype(jnp.float32),
                    )
                    mean = jnp.mean(wide * wide, -1, keepdims=True)
                    at = (c * 2 + h) * page.shape[1]
                    into = pl.ds(pl.multiple_of(at + i * 16, 16), 16)
                    normed[into, :] = (wide * lax.rsqrt(mean + norm_eps) * gain[...]).astype(
                        jnp.bfloat16
                    )
                    return carry

                lax.fori_loop(0, page.shape[1] // 16, norm, 0)

        def multiply(i, total):
            part = pl.ds(pl.multiple_of(i * per_step, per_step), per_step)
            slabs = weights[pl.ds(i * (per_step // depth), per_step // depth)]
            return total + jnp.dot(
                normed[:, part],
                slabs.reshape(per_step, slab.shape[3]),
                preferred_element_type=jnp.float32,
            )

        projected = lax.fori_loop(
            0, 4, multiply, jnp.zeros((pair_count, slab.shape[3]), jnp.float32)
        )
        start_column = jnp.concatenate(columns, 0)
        rows = pl.ds(pl.multiple_of(pair * pair_count, pair_count), pair_count)
        first = block * queries.shape[0] + pair * pair_count
        position = first + lax.broadcasted_iota(jnp.int32, (pair_count, 1), 0)
        begin = start_column.astype(jnp.int32)
        starts[rows, :] = begin
        angles = (position - begin).astype(jnp.float32) * freq[...]
        cosine, sine = jnp.cos(angles), jnp.sin(angles)
        for head in range(query_width // HEAD_SIZE):
            part = slice(head * HEAD_SIZE, (head + 1) * HEAD_SIZE)
            queries[rows, part] = rotated(projected[:, part], cosine, sine)
        keys[rows, :] = rotated(
            projected[:, query_width : query_width + HEAD_SIZE], cosine, sine
        )
        values[rows, :] = projected[:, query_width + HEAD_SIZE :].astype(jnp.bfloat16)

    def pick_sinks():
        found = seg_starts()
        count = NSEG * SINKS

        def spread_out(shape, axis):
            place = lax.broadcasted_iota(jnp.int32, shape, axis)
            begin = jnp.zeros(shape, jnp.float32)
            for segment in range(NSEG):
                inside = (place >= segment * SINKS) & (place < (segment + 1) * SINKS)
                begin = jnp.where(inside, found[segment], begin)
            begin = begin.astype(jnp.int32)
            return begin, begin + place % SINKS

        begin, place = spread_out((1, count), 1)
        sink_rows[0:1, :] = place
        sink_rows[1:2, :] = begin
        place = spread_out((count, 1), 0)[1] - block * queries.shape[0]
        chosen = lax.broadcasted_iota(jnp.int32, (count, queries.shape[0]), 1) == place
        chosen = chosen.astype(jnp.float32).astype(jnp.bfloat16)
        for i, source in enumerate((keys, values)):
            sink_pairs[i] = jnp.dot(
                chosen, source[...], preferred_element_type=jnp.float32
            ).astype(jnp.bfloat16)

    own_copies = [
        pltpu.make_async_copy(page, pages.at[z, core], local.at[0]),
        pltpu.make_async_copy(slab, weights.at[x * 4 + y], local.at[1]),
        pltpu.make_async_copy(note, notes.at[y, x, q], local.at[2]),
    ]
    for c in own_copies:
        c.start()
    for r in range(1, 8):
        start(("note", r), note, notes.at[y, x, q], group[r - 1])
    for order in range(2):
        for d in (1, -1):
            start(("w1", order, d), slab.at[order], origin(order, 0, 0), towards(order, d, 0))
    for h in range(2):
        for d in (1, -1):
            start(("z", d, 0, h), page.at[h], page_at(0, h, core), ring[d])
    for order in range(2):
        for d in (1, -1):
            start(("w2", order, 0, d), slab.at[order], origin(order, 0, 0), towards(order, 0, d))
    for h in range(2):
        start(("c", 0, 0, h), page.at[h], page_at(0, h, core), partner)

    def page_step(s, h):
        for d in (1, -1):
            if s == 3 and h != (0 if d == 1 else 1):
                continue
            at = page_at(-d * (s + 1), h, core)
            arrived(("z", d, s, h), at)
            if s + 1 < 3 or (s + 1 == 3 and h == (0 if d == 1 else 1)):
                start(("z", d, s + 1, h), at, at, ring[d])
            start(("c", d, s, h), at, at, partner)

    def second_send(order, k):
        for d in (1, -1):
            start(("w2", order, k, d), origin(order, k, 0), origin(order, k, 0), towards(order, 0, d))

    def second_relay(order, k):
        for d in (1, -1):
            at = origin(order, k, -d)
            arrived(("w2", order, k, d), at)
            half = at.at[0 if d == 1 else 1]
            start(("w2r", order, k, d), half, half, towards(order, 0, d))

    for r in range(1, 8):
        arrived(("note", r), notes.at[y, x, (q + 8 - r) % 8])
    own_copies[2].wait()
    for r in range(1, 4):
        start(("notex", r), notes.at[y, x], notes.at[y, x], columns[r - 1])
    for order in range(2):
        for d in (1, -1):
            at = origin(order, -d, 0)
            arrived(("w1", order, d), at)
            half = at.at[0 if d == 1 else 1]
            start(("w1r", order, d), half, half, towards(order, d, 0))
            second_send(order, -d)
    for order in range(2):
        second_relay(order, 0)
    for r in range(1, 4):
        arrived(("notex", r), notes.at[y, (x + 4 - r) % 4])
    for r in range(1, 4):
        start(("notey", r), notes.at[y], notes.at[y], lines[r - 1])
    page_step(0, 0)
    for order in range(2):
        for d in (1, -1):
            arrived(("w1r", order, d), origin(order, -2 * d, 0).at[0 if d == 1 else 1])
        second_send(order, 2)
    for order in range(2):
        second_relay(order, -1)
        second_relay(order, 1)
    page_step(0, 1)
    for order in range(2):
        second_relay(order, 2)
    page_step(1, 0)
    for r in range(1, 4):
        arrived(("notey", r), notes.at[(y + 4 - r) % 4])
    for order in range(2):
        for k in (0, -1, 1, 2):
            for d in (1, -1):
                arrived(("w2r", order, k, d), origin(order, k, -2 * d).at[0 if d == 1 else 1])
    page_step(1, 1)

    def passed(s):
        for h in range(2):
            for d in (1, -1):
                if s < 3 or h == (0 if d == 1 else 1):
                    arrived(("c", d, s, h), page_at(-d * (s + 1), h, 1 - core))

    own_copies[0].wait()
    own_copies[1].wait()
    for h in range(2):
        arrived(("c", 0, 0, h), page_at(0, h, 1 - core))
    passed(0)
    project(0)
    page_step(2, 0)
    passed(1)
    project(3 - 2 * dp)
    page_step(2, 1)
    passed(2)
    project(1 + 2 * dp)
    page_step(3, 0)
    page_step(3, 1)
    passed(3)
    project(2)
    pick_sinks()
    for c in started:
        c.wait_send()


COPIES = 7 + 3 + 3 + 14 + 16 + 4 + 4 + 16 + 16


def gather(page, slab, note, gain, freq):
    rows, width = page.shape
    depth, columns = slab.shape
    block_rows = KEY_VALUE_HEADS * rows
    vmem = pl.BlockSpec(memory_space=pltpu.VMEM)
    head_rows = jax.ShapeDtypeStruct((block_rows, HEAD_SIZE), page.dtype)
    return pl.pallas_call(
        gather_kernel,
        out_shape=(
            jax.ShapeDtypeStruct((block_rows, columns - 2 * HEAD_SIZE), page.dtype),
            head_rows,
            head_rows,
            jax.ShapeDtypeStruct((block_rows, 1), jnp.int32),
            jax.ShapeDtypeStruct((2, NSEG * SINKS), jnp.int32),
            jax.ShapeDtypeStruct((2, NSEG * SINKS, HEAD_SIZE), page.dtype),
        ),
        in_specs=[vmem] * 5,
        out_specs=(vmem,) * 6,
        scratch_shapes=[
            pltpu.VMEM((8, 2, 2, rows // 2, width), page.dtype),
            pltpu.VMEM((16, 2, 2, depth // 4, columns), slab.dtype),
            pltpu.VMEM((4, 4, 8, 1, note.shape[0]), note.dtype),
            pltpu.VMEM((2 * rows, width), page.dtype),
            pltpu.SemaphoreType.DMA((COPIES,)),
            pltpu.SemaphoreType.DMA((COPIES,)),
            pltpu.SemaphoreType.DMA((3,)),
        ],
        compiler_params=pltpu.CompilerParams(collective_id=0, has_side_effects=True),
        name="gather",
    )(
        page.reshape(2, rows // 2, width),
        slab.reshape(2, 2, depth // 4, columns),
        note.reshape(1, -1),
        gain.reshape(1, -1),
        freq.reshape(1, -1),
    )


PAGE_ROWS = 128
REACH = WINDOW + PAGE_ROWS
CONTEXT_COPIES = 16
ATTEND_COPIES = CONTEXT_COPIES + 2 + 15 + 16 + 4
FAR = 2


def attend_kernel(
    queries,
    keys,
    values,
    starts,
    sink_rows,
    sink_pairs,
    context,
    key_out,
    value_out,
    key_window,
    value_window,
    sinks,
    mixed,
    passing,
    send,
    recv,
    local,
):
    dp = lax.axis_index("dp")
    t = lax.axis_index("tensor")
    core, zh = t % 2, (t // 2) % 4
    q, block = t % 8, t // 8
    width = mixed.shape[2]

    def copy(i, src, dst, target):
        return pltpu.make_async_remote_copy(
            src_ref=src,
            dst_ref=dst,
            send_sem=send.at[i],
            recv_sem=recv.at[i],
            device_id=target,
            device_id_type=pl.DeviceIdType.MESH,
        )

    def head(r):
        return (dp, block * 8 + (q + r) % 8)

    def page_near(shift, flip):
        return ((zh + shift) % 4) * 2 + (core + flip) % 2

    partner = (1 - dp, t)

    def plane(r):
        return (dp, ((block + r) % 16) * 8 + q)

    peers = [head(r) for r in range(1, 8)] + [plane(r) for r in range(1, 16)]
    peers += [(1 - dp, block * 8 + (q + r) % 8) for r in range(8)]
    barrier = pltpu.get_barrier_semaphore()
    for peer in peers:
        pl.semaphore_signal(barrier, inc=1, device_id=peer, device_id_type=pl.DeviceIdType.MESH)
    pl.semaphore_wait(barrier, len(peers))

    own_rows = pl.ds(WINDOW, keys.shape[0])
    last_rows = pl.ds(keys.shape[0] - WINDOW, WINDOW)
    first_rows = pl.ds(0, WINDOW)

    def page_rows(page):
        return pl.ds(pl.multiple_of(page * PAGE_ROWS, PAGE_ROWS), PAGE_ROWS)

    at = CONTEXT_COPIES
    sent = []
    for i, (source, target) in enumerate(((keys, key_window), (values, value_window))):
        c = copy(at + i, source.at[last_rows], target.at[first_rows], plane(1))
        c.start()
        sent.append(c)
    at += 2
    for r in range(1, 16):
        c = copy(at + r - 1, sink_pairs, sinks.at[block], plane(r))
        c.start()
        sent.append(c)
    locals_now = [
        pltpu.make_async_copy(keys, key_window.at[own_rows], local.at[0]),
        pltpu.make_async_copy(values, value_window.at[own_rows], local.at[1]),
        pltpu.make_async_copy(sink_pairs, sinks.at[block], local.at[2]),
        pltpu.make_async_copy(keys.at[page_rows(q)], key_out.at[q], local.at[3]),
        pltpu.make_async_copy(values.at[page_rows(q)], value_out.at[q], local.at[4]),
    ]
    for c in locals_now:
        c.start()
    caches = ((keys, key_out), (values, value_out))
    spread = [(shift, flip) for shift in (FAR, 3, 1, 0) for flip in (1, 0)][:7]

    def cache_slot(shift, flip, i):
        return CONTEXT_COPIES + 17 + (shift * 2 + flip) * 2 + i

    def passing_slot(flip, i):
        return CONTEXT_COPIES + 33 + flip * 2 + i

    for shift, flip in spread:
        page = page_near(shift, flip)
        for i, (source, target) in enumerate(caches):
            piece = source.at[page_rows(page)]
            if shift == FAR:
                c = copy(
                    passing_slot(flip, i), piece, passing.at[i, flip], (1 - dp, block * 8 + page)
                )
            else:
                c = copy(cache_slot(shift, flip, i), piece, target.at[q], (dp, block * 8 + page))
            c.start()
            sent.append(c)

    def hand_on(flip, i):
        piece = passing.at[i, flip]
        source = page_near(4 - FAR, flip)
        return copy(cache_slot(FAR, flip, i), piece, caches[i][1].at[source], partner)

    at = CONTEXT_COPIES
    for i, target in enumerate((key_window, value_window)):
        copy(at + i, target.at[first_rows], target.at[first_rows], plane(1)).wait_recv()
    at += 2
    for r in range(1, 16):
        landed = sinks.at[(block + 16 - r) % 16]
        copy(at + r - 1, landed, landed, plane(1)).wait_recv()
    for c in locals_now[:3]:
        c.wait()

    sink_sum = jnp.sum(sinks[...].astype(jnp.float32), 0).astype(jnp.bfloat16)
    sink_keys, sink_values = sink_sum[0], sink_sum[1]
    scale = HEAD_SIZE ** (-0.5)
    last_dims = (((1,), (1,)), ((), ()))

    def page_of(step):
        turn = step // 2
        return page_near(FAR + turn * (turn + 1) // 2, 1 + step)

    def columns(head_index):
        return pl.ds(pl.multiple_of(head_index * width, width), width)

    def to_half(step, half):
        target = context.at[dp, :, columns(q)]
        i = step if half == 0 else 8 + step
        side = dp if half == 0 else 1 - dp
        return copy(i, mixed.at[step], target, (side, block * 8 + page_of(step)))

    def attend(step, carry):
        page = page_of(step)
        rows = page_rows(page)
        row_start = starts[rows, :]
        first = block * keys.shape[0] + page * PAGE_ROWS
        query_pos = first + lax.broadcasted_iota(jnp.int32, (PAGE_ROWS, 1), 0)
        key_pos = first - WINDOW + lax.broadcasted_iota(jnp.int32, (PAGE_ROWS, REACH), 1)
        allowed = (
            (key_pos <= query_pos) & (key_pos >= row_start) & (key_pos >= query_pos - WINDOW)
        )
        sink_pos = sink_rows[0:1, :]
        sink_allowed = (
            (sink_rows[1:2, :] == row_start)
            & (sink_pos <= query_pos)
            & (sink_pos < query_pos - WINDOW)
        )
        reach = pl.ds(pl.multiple_of(page * PAGE_ROWS, PAGE_ROWS), REACH)
        near_keys = key_window[reach, :]
        near_values = value_window[reach, :]
        for h in range(width // HEAD_SIZE):
            part = pl.ds(h * HEAD_SIZE, HEAD_SIZE)
            query = queries[rows, part]
            scores = (
                lax.dot_general(query, near_keys, last_dims, preferred_element_type=jnp.float32)
                * scale
            )
            sink_scores = (
                lax.dot_general(query, sink_keys, last_dims, preferred_element_type=jnp.float32)
                * scale
            )
            scores = jnp.where(allowed, scores, -jnp.inf)
            sink_scores = jnp.where(sink_allowed, sink_scores, -jnp.inf)
            top = jnp.maximum(
                jnp.max(scores, -1, keepdims=True), jnp.max(sink_scores, -1, keepdims=True)
            )
            near = jnp.exp(scores - top)
            far = jnp.exp(sink_scores - top)
            inverse = 1.0 / (
                jnp.sum(near, -1, keepdims=True) + jnp.sum(far, -1, keepdims=True)
            )
            result = jnp.dot(
                (near * inverse).astype(jnp.bfloat16),
                near_values,
                preferred_element_type=jnp.float32,
            ) + jnp.dot(
                (far * inverse).astype(jnp.bfloat16),
                sink_values,
                preferred_element_type=jnp.float32,
            )
            mixed[step, :, part] = result.astype(jnp.bfloat16)

        @pl.when(step > 0)
        def _():
            to_half(step - 1, 1).start()

        @pl.when(step > 2)
        def _():
            to_half(step - 1, 0).start()

        @pl.when(step == 2)
        def _():
            for flip in range(2):
                for i in range(2):
                    piece = passing.at[i, flip]
                    copy(passing_slot(flip, i), piece, piece, partner).wait_recv()
                    hand_on(flip, i).start()

        return carry

    lax.fori_loop(0, 8, attend, 0)
    own = pltpu.make_async_copy(mixed.at[7], context.at[dp, :, columns(q)], local.at[5])
    own.start()
    to_half(7, 1).start()

    def source_of(step):
        turn = step // 2
        return page_near(8 - FAR - turn * (turn + 1) // 2, 1 + step)

    def landed(step, half):
        return context.at[dp if half == 0 else 1 - dp, :, columns(source_of(step))]

    def pass_context(step):
        piece = landed(step, 1)
        return copy(step, piece, piece, partner)

    for step in range(2):
        copy(8 + step, landed(step, 1), landed(step, 1), partner).wait_recv()
        pass_context(step).start()
    for shift, flip in spread:
        source = page_near(4 - shift, flip)
        for i in range(2):
            piece = caches[i][1].at[source]
            copy(cache_slot(shift, flip, i), piece, piece, partner).wait_recv()
    for step in range(2, 8):
        copy(8 + step, landed(step, 1), landed(step, 1), partner).wait_recv()
    for step in range(7):
        copy(step, landed(step, 0), landed(step, 0), partner).wait_recv()
    for c in sent + [hand_on(flip, i) for flip in range(2) for i in range(2)]:
        c.wait_send()
    for c in locals_now[3:]:
        c.wait()
    for step in range(8):
        if step < 2:
            pass_context(step).wait_send()
        elif step < 7:
            to_half(step, 0).wait_send()
        to_half(step, 1).wait_send()
    own.wait()


def attend_pages(queries, keys, values, starts, sink_rows, sink_pairs):
    rows, width = queries.shape
    vmem = pl.BlockSpec(memory_space=pltpu.VMEM)
    hbm = pl.BlockSpec(memory_space=pltpu.HBM)
    cache = jax.ShapeDtypeStruct((KEY_VALUE_HEADS, PAGE_ROWS, HEAD_SIZE), keys.dtype)
    return pl.pallas_call(
        attend_kernel,
        out_shape=(
            jax.ShapeDtypeStruct((2, PAGE_ROWS, KEY_VALUE_HEADS * width), queries.dtype),
            cache,
            cache,
        ),
        in_specs=[vmem] * 6,
        out_specs=(hbm,) * 3,
        scratch_shapes=[
            pltpu.VMEM((WINDOW + rows, HEAD_SIZE), keys.dtype),
            pltpu.VMEM((WINDOW + rows, HEAD_SIZE), keys.dtype),
            pltpu.VMEM((16,) + sink_pairs.shape, sink_pairs.dtype),
            pltpu.VMEM((8, PAGE_ROWS, width), queries.dtype),
            pltpu.VMEM((2, 2, PAGE_ROWS, HEAD_SIZE), keys.dtype),
            pltpu.SemaphoreType.DMA((ATTEND_COPIES,)),
            pltpu.SemaphoreType.DMA((ATTEND_COPIES,)),
            pltpu.SemaphoreType.DMA((6,)),
        ],
        compiler_params=pltpu.CompilerParams(collective_id=1, has_side_effects=True),
        name="attend",
    )(queries, keys, values, starts, sink_rows, sink_pairs)


def body(tokens, norm_gain, segments, deal_table, projection):
    group_id = lax.axis_index("dp")
    owner_group = jnp.sum(jnp.where(jnp.arange(deal_table.shape[1]) == group_id, deal_table[0], 0))
    client = jnp.where(owner_group == group_id, group_id, 1 - group_id).astype(jnp.int32)
    note = jnp.concatenate((segments[0], jnp.broadcast_to(client, segments[0].shape)))
    rope_freq = rope_base ** (-(jnp.arange(0, HEAD_SIZE, 2).astype(jnp.float32) / HEAD_SIZE))
    attended = gather(tokens[0], projection, note, norm_gain, rope_freq)
    contexts, key_cache, value_cache = attend_pages(*attended)
    context = jnp.where(owner_group == 1, contexts[1], contexts[0])
    return (context[None], key_cache[None], value_cache[None])


def solution(mesh):
    placed = (P("dp", "tensor", None), P(), P("dp", "tensor"), P("tensor", None), P("tensor", None))
    return jax.shard_map(
        body,
        mesh=mesh,
        in_specs=placed,
        out_specs=(
            P("dp", "tensor", None),
            P("dp", None, "tensor", None),
            P("dp", None, "tensor", None),
        ),
        check_vma=False,
    )
```

```python
import jax
import jax.numpy as jnp
from jax import lax
from jax.experimental import pallas as pl
from jax.experimental.pallas import tpu as pltpu
from jax.sharding import PartitionSpec as P

QUERY_HEADS = 32
KEY_VALUE_HEADS = 8
HEAD_SIZE = 128
NSEG = 8
WINDOW = 512
SINKS = 4


rope_base = 500000.0
norm_eps = 1e-05


def kernel(
    page,
    slab,
    note,
    gain,
    freq,
    context,
    key_out,
    value_out,
    pages,
    weights,
    notes,
    normed,
    queries,
    starts,
    sink_rows,
    sink_pairs,
    key_window,
    value_window,
    sinks,
    mixed,
    passing,
    send,
    recv,
    local,
    send_mixed,
    recv_mixed,
    local_mixed,
):
    keys = key_window.at[pl.ds(WINDOW, queries.shape[0])]
    values = value_window.at[pl.ds(WINDOW, queries.shape[0])]
    meet()
    send_cache, send_edges, attend_all = attention(
        queries,
        keys,
        values,
        starts,
        sink_rows,
        sink_pairs,
        context,
        key_out,
        value_out,
        key_window,
        value_window,
        sinks,
        mixed,
        passing,
        send_mixed,
        recv_mixed,
        local_mixed,
    )
    dp = lax.axis_index("dp")
    t = lax.axis_index("tensor")
    core, zh = t % 2, (t // 2) % 4
    y, x = (t // 8) % 4, t // 32
    z = zh * 2 + dp
    q = t % 8

    def device(dx, dy, z_at, core_at):
        z_at = z_at % 8
        block = ((x + dx) % 4) * 4 + (y + dy) % 4
        return (z_at % 2, (block * 4 + z_at // 2) * 2 + core_at)

    slots = {}

    def copy(key, src, dst, target):
        i = slots.setdefault(key, len(slots))
        return pltpu.make_async_remote_copy(
            src_ref=src,
            dst_ref=dst,
            send_sem=send.at[i],
            recv_sem=recv.at[i],
            device_id=target,
            device_id_type=pl.DeviceIdType.MESH,
        )

    started = []

    def start(key, src, dst, target):
        c = copy(key, src, dst, target)
        c.start()
        started.append(c)

    partner = (dp, t + 1 - 2 * core)

    def arrived(key, dst):
        copy(key, dst, dst, partner).wait_recv()

    group = [(dp, (t // 8) * 8 + (q + r) % 8) for r in range(1, 8)]
    columns = [device(r, 0, z, core) for r in range(1, 4)]
    lines = [device(0, r, z, core) for r in range(1, 4)]
    ring = {1: device(0, 0, z + 1, core), -1: device(0, 0, z + 7, core)}
    def page_at(dz, h, c):
        return pages.at[(z + dz + 8) % 8, c, h]

    def origin(order, da, db):
        dx, dy = (da, db) if order == 0 else (db, da)
        return weights.at[((x + dx + 4) % 4) * 4 + (y + dy + 4) % 4, order]

    def towards(order, da, db):
        dx, dy = (da, db) if order == 0 else (db, da)
        return device(dx + 4, dy + 4, z, core)

    page_count = 2 * page.shape[1]
    pair_count = 2 * page_count
    model_width = page.shape[2]
    query_width = queries.shape[1]
    depth = 4 * slab.shape[2]
    per_step = model_width // 4
    block = x * 4 + y

    def seg_starts():
        ids = notes[:, :, :, :, 0:page_count]
        found = []
        for segment in range(NSEG):
            below = jnp.sum((ids < segment).astype(jnp.float32), (0, 1, 2))
            found.append(jnp.sum(below, -1, keepdims=True))
        return found

    def rotated(block_values, cosine, sine):
        half = HEAD_SIZE // 2
        first, second = block_values[:, :half], block_values[:, half:]
        return jnp.concatenate(
            (first * cosine - second * sine, second * cosine + first * sine), -1
        ).astype(jnp.bfloat16)

    def project(shift):
        pair = (zh + shift) % 4
        found = seg_starts()
        eye = lax.broadcasted_iota(jnp.int32, (page_count, page_count), 0)
        eye = eye == lax.broadcasted_iota(jnp.int32, (page_count, page_count), 1)
        columns = []
        for c in range(2):
            told = notes[y, x, pair * 2 + c]
            ids, client = told[:, :page_count], told[:, page_count:]
            start_row = jnp.zeros(ids.shape, jnp.float32)
            for segment in range(NSEG):
                start_row = jnp.where(ids == segment, found[segment], start_row)
            start_row = jnp.broadcast_to(start_row, (page_count, page_count))
            columns.append(jnp.sum(jnp.where(eye, start_row, 0.0), 1, keepdims=True))
            upper = jnp.tile(client, (1, model_width // page_count)) == 1
            upper = jnp.broadcast_to(upper, (16, model_width))
            for h in range(2):

                def norm(i, carry, c=c, h=h, upper=upper):
                    rows = pl.ds(pl.multiple_of(i * 16, 16), 16)
                    wide = jnp.where(
                        upper,
                        pages[pair * 2 + 1, c, h, rows, :].astype(jnp.float32),
                        pages[pair * 2, c, h, rows, :].astype(jnp.float32),
                    )
                    mean = jnp.mean(wide * wide, -1, keepdims=True)
                    at = (c * 2 + h) * page.shape[1]
                    into = pl.ds(pl.multiple_of(at + i * 16, 16), 16)
                    normed[into, :] = (wide * lax.rsqrt(mean + norm_eps) * gain[...]).astype(
                        jnp.bfloat16
                    )
                    return carry

                lax.fori_loop(0, page.shape[1] // 16, norm, 0)

        def multiply(i, total):
            part = pl.ds(pl.multiple_of(i * per_step, per_step), per_step)
            slabs = weights[pl.ds(i * (per_step // depth), per_step // depth)]
            return total + jnp.dot(
                normed[:, part],
                slabs.reshape(per_step, slab.shape[3]),
                preferred_element_type=jnp.float32,
            )

        projected = lax.fori_loop(
            0, 4, multiply, jnp.zeros((pair_count, slab.shape[3]), jnp.float32)
        )
        start_column = jnp.concatenate(columns, 0)
        rows = pl.ds(pl.multiple_of(pair * pair_count, pair_count), pair_count)
        first = block * queries.shape[0] + pair * pair_count
        position = first + lax.broadcasted_iota(jnp.int32, (pair_count, 1), 0)
        begin = start_column.astype(jnp.int32)
        starts[rows, :] = begin
        angles = (position - begin).astype(jnp.float32) * freq[...]
        cosine, sine = jnp.cos(angles), jnp.sin(angles)
        for head in range(query_width // HEAD_SIZE):
            part = slice(head * HEAD_SIZE, (head + 1) * HEAD_SIZE)
            queries[rows, part] = rotated(projected[:, part], cosine, sine)
        keys[rows, :] = rotated(
            projected[:, query_width : query_width + HEAD_SIZE], cosine, sine
        )
        values[rows, :] = projected[:, query_width + HEAD_SIZE :].astype(jnp.bfloat16)

    def pick_sinks():
        found = seg_starts()
        count = NSEG * SINKS

        def spread_out(shape, axis):
            place = lax.broadcasted_iota(jnp.int32, shape, axis)
            begin = jnp.zeros(shape, jnp.float32)
            for segment in range(NSEG):
                inside = (place >= segment * SINKS) & (place < (segment + 1) * SINKS)
                begin = jnp.where(inside, found[segment], begin)
            begin = begin.astype(jnp.int32)
            return begin, begin + place % SINKS

        begin, place = spread_out((1, count), 1)
        sink_rows[0:1, :] = place
        sink_rows[1:2, :] = begin
        place = spread_out((count, 1), 0)[1] - block * queries.shape[0]
        chosen = lax.broadcasted_iota(jnp.int32, (count, queries.shape[0]), 1) == place
        chosen = chosen.astype(jnp.float32).astype(jnp.bfloat16)
        for i, source in enumerate((keys, values)):
            sink_pairs[i] = jnp.dot(
                chosen, source[...], preferred_element_type=jnp.float32
            ).astype(jnp.bfloat16)

    own_copies = [
        pltpu.make_async_copy(page, pages.at[z, core], local.at[0]),
        pltpu.make_async_copy(slab, weights.at[x * 4 + y], local.at[1]),
        pltpu.make_async_copy(note, notes.at[y, x, q], local.at[2]),
    ]
    for c in own_copies:
        c.start()
    for r in range(1, 8):
        start(("note", r), note, notes.at[y, x, q], group[r - 1])
    for order in range(2):
        for d in (1, -1):
            start(("w1", order, d), slab.at[order], origin(order, 0, 0), towards(order, d, 0))
    for h in range(2):
        for d in (1, -1):
            start(("z", d, 0, h), page.at[h], page_at(0, h, core), ring[d])
    for order in range(2):
        for d in (1, -1):
            start(("w2", order, 0, d), slab.at[order], origin(order, 0, 0), towards(order, 0, d))
    for h in range(2):
        start(("c", 0, 0, h), page.at[h], page_at(0, h, core), partner)

    def page_step(s, h):
        for d in (1, -1):
            if s == 3 and h != (0 if d == 1 else 1):
                continue
            at = page_at(-d * (s + 1), h, core)
            arrived(("z", d, s, h), at)
            if s + 1 < 3 or (s + 1 == 3 and h == (0 if d == 1 else 1)):
                start(("z", d, s + 1, h), at, at, ring[d])
            start(("c", d, s, h), at, at, partner)

    def second_send(order, k):
        for d in (1, -1):
            start(("w2", order, k, d), origin(order, k, 0), origin(order, k, 0), towards(order, 0, d))

    def second_relay(order, k):
        for d in (1, -1):
            at = origin(order, k, -d)
            arrived(("w2", order, k, d), at)
            half = at.at[0 if d == 1 else 1]
            start(("w2r", order, k, d), half, half, towards(order, 0, d))

    for r in range(1, 8):
        arrived(("note", r), notes.at[y, x, (q + 8 - r) % 8])
    own_copies[2].wait()
    for r in range(1, 4):
        start(("notex", r), notes.at[y, x], notes.at[y, x], columns[r - 1])
    for order in range(2):
        for d in (1, -1):
            at = origin(order, -d, 0)
            arrived(("w1", order, d), at)
            half = at.at[0 if d == 1 else 1]
            start(("w1r", order, d), half, half, towards(order, d, 0))
            second_send(order, -d)
    for order in range(2):
        second_relay(order, 0)
    for r in range(1, 4):
        arrived(("notex", r), notes.at[y, (x + 4 - r) % 4])
    for r in range(1, 4):
        start(("notey", r), notes.at[y], notes.at[y], lines[r - 1])
    page_step(0, 0)
    for order in range(2):
        for d in (1, -1):
            arrived(("w1r", order, d), origin(order, -2 * d, 0).at[0 if d == 1 else 1])
        second_send(order, 2)
    for order in range(2):
        second_relay(order, -1)
        second_relay(order, 1)
    page_step(0, 1)
    for order in range(2):
        second_relay(order, 2)
    page_step(1, 0)
    for r in range(1, 4):
        arrived(("notey", r), notes.at[(y + 4 - r) % 4])
    for order in range(2):
        for k in (0, -1, 1, 2):
            for d in (1, -1):
                arrived(("w2r", order, k, d), origin(order, k, -2 * d).at[0 if d == 1 else 1])
    page_step(1, 1)

    def passed(s):
        for h in range(2):
            for d in (1, -1):
                if s < 3 or h == (0 if d == 1 else 1):
                    arrived(("c", d, s, h), page_at(-d * (s + 1), h, 1 - core))

    own_copies[0].wait()
    own_copies[1].wait()
    for h in range(2):
        arrived(("c", 0, 0, h), page_at(0, h, 1 - core))
    passed(0)
    project(0)
    page_step(2, 0)
    passed(1)
    project(3 - 2 * dp)
    page_step(2, 1)
    send_cache(0)
    send_cache(3 - 2 * dp)
    passed(2)
    project(1 + 2 * dp)
    page_step(3, 0)
    page_step(3, 1)
    send_cache(1 + 2 * dp)
    passed(3)
    project(FAR)
    pick_sinks()
    send_edges()
    attend_all()
    for c in started:
        c.wait_send()


COPIES = 7 + 3 + 3 + 14 + 16 + 4 + 4 + 16 + 16


PAGE_ROWS = 128
REACH = WINDOW + PAGE_ROWS
CONTEXT_COPIES = 16
ATTEND_COPIES = CONTEXT_COPIES + 2 + 15 + 16 + 4
FAR = 2


def meet():
    dp = lax.axis_index("dp")
    t = lax.axis_index("tensor")
    q, block = t % 8, t // 8
    peers = [(dp, block * 8 + (q + r) % 8) for r in range(1, 8)]
    peers += [(dp, ((block + r) % 16) * 8 + q) for r in range(1, 16)]
    peers += [(1 - dp, block * 8 + (q + r) % 8) for r in range(8)]
    barrier = pltpu.get_barrier_semaphore()
    for peer in peers:
        pl.semaphore_signal(barrier, inc=1, device_id=peer, device_id_type=pl.DeviceIdType.MESH)
    pl.semaphore_wait(barrier, len(peers))


def attention(
    queries,
    keys,
    values,
    starts,
    sink_rows,
    sink_pairs,
    context,
    key_out,
    value_out,
    key_window,
    value_window,
    sinks,
    mixed,
    passing,
    send,
    recv,
    local,
):
    dp = lax.axis_index("dp")
    t = lax.axis_index("tensor")
    core, zh = t % 2, (t // 2) % 4
    q, block = t % 8, t // 8
    width = mixed.shape[2]

    def copy(i, src, dst, target):
        return pltpu.make_async_remote_copy(
            src_ref=src,
            dst_ref=dst,
            send_sem=send.at[i],
            recv_sem=recv.at[i],
            device_id=target,
            device_id_type=pl.DeviceIdType.MESH,
        )

    def plane(r):
        return (dp, ((block + r) % 16) * 8 + q)

    def page_near(shift, flip):
        return ((zh + shift) % 4) * 2 + (core + flip) % 2

    partner = (1 - dp, t)
    last_rows = pl.ds(keys.shape[0] - WINDOW, WINDOW)
    first_rows = pl.ds(0, WINDOW)

    def page_rows(page):
        return pl.ds(pl.multiple_of(page * PAGE_ROWS, PAGE_ROWS), PAGE_ROWS)

    sent = []
    own_copies = [
        pltpu.make_async_copy(sink_pairs, sinks.at[block], local.at[0]),
        pltpu.make_async_copy(keys.at[page_rows(q)], key_out.at[q], local.at[1]),
        pltpu.make_async_copy(values.at[page_rows(q)], value_out.at[q], local.at[2]),
    ]
    edge_slot, sink_slot = CONTEXT_COPIES, CONTEXT_COPIES + 2
    caches = ((keys, key_out), (values, value_out))
    spread = [(shift, flip) for shift in (FAR, 3, 1, 0) for flip in (1, 0)][:7]

    def cache_slot(shift, flip, i):
        return CONTEXT_COPIES + 17 + (shift * 2 + flip) * 2 + i

    def passing_slot(flip, i):
        return CONTEXT_COPIES + 33 + flip * 2 + i

    def send_cache(shift):
        own = isinstance(shift, int) and shift == 0
        far = isinstance(shift, int) and shift == FAR
        for flip in (1,) if own else (1, 0):
            page = page_near(shift, flip)
            for i, (source, target) in enumerate(caches):
                piece = source.at[page_rows(page)]
                if far:
                    c = copy(
                        passing_slot(flip, i),
                        piece,
                        passing.at[i, flip],
                        (1 - dp, block * 8 + page),
                    )
                else:
                    c = copy(
                        cache_slot(shift, flip, i), piece, target.at[q], (dp, block * 8 + page)
                    )
                c.start()
                sent.append(c)

    def send_edges():
        for i, (source, target) in enumerate(((keys, key_window), (values, value_window))):
            c = copy(
                edge_slot + i, source.at[last_rows], target.at[first_rows], plane(1)
            )
            c.start()
            sent.append(c)
        send_cache(FAR)
        for c in own_copies[1:]:
            c.start()
        for r in range(1, 16):
            c = copy(sink_slot + r - 1, sink_pairs, sinks.at[block], plane(r))
            c.start()
            sent.append(c)
        own_copies[0].start()

    def hand_on(flip, i):
        piece = passing.at[i, flip]
        source = page_near(4 - FAR, flip)
        return copy(cache_slot(FAR, flip, i), piece, caches[i][1].at[source], partner)

    def attend_all():
        for i, target in enumerate((key_window, value_window)):
            copy(edge_slot + i, target.at[first_rows], target.at[first_rows], plane(1)).wait_recv()
        for r in range(1, 16):
            landed = sinks.at[(block + 16 - r) % 16]
            copy(sink_slot + r - 1, landed, landed, plane(1)).wait_recv()
        own_copies[0].wait()

        sink_sum = jnp.sum(sinks[...].astype(jnp.float32), 0).astype(jnp.bfloat16)
        sink_keys, sink_values = sink_sum[0], sink_sum[1]
        scale = HEAD_SIZE ** (-0.5)
        last_dims = (((1,), (1,)), ((), ()))

        def page_of(step):
            turn = step // 2
            return page_near(FAR + turn * (turn + 1) // 2, 1 + step)

        def columns(head_index):
            return pl.ds(pl.multiple_of(head_index * width, width), width)

        def to_half(step, half):
            target = context.at[dp, :, columns(q)]
            i = step if half == 0 else 8 + step
            side = dp if half == 0 else 1 - dp
            return copy(i, mixed.at[step], target, (side, block * 8 + page_of(step)))

        def attend(step, carry):
            page = page_of(step)
            rows = page_rows(page)
            row_start = starts[rows, :]
            first = block * keys.shape[0] + page * PAGE_ROWS
            query_pos = first + lax.broadcasted_iota(jnp.int32, (PAGE_ROWS, 1), 0)
            key_pos = first - WINDOW + lax.broadcasted_iota(jnp.int32, (PAGE_ROWS, REACH), 1)
            allowed = (
                (key_pos <= query_pos) & (key_pos >= row_start) & (key_pos >= query_pos - WINDOW)
            )
            sink_pos = sink_rows[0:1, :]
            sink_allowed = (
                (sink_rows[1:2, :] == row_start)
                & (sink_pos <= query_pos)
                & (sink_pos < query_pos - WINDOW)
            )
            reach = pl.ds(pl.multiple_of(page * PAGE_ROWS, PAGE_ROWS), REACH)
            near_keys = key_window[reach, :]
            near_values = value_window[reach, :]
            for h in range(width // HEAD_SIZE):
                part = pl.ds(h * HEAD_SIZE, HEAD_SIZE)
                query = queries[rows, part]
                scores = (
                    lax.dot_general(query, near_keys, last_dims, preferred_element_type=jnp.float32)
                    * scale
                )
                sink_scores = (
                    lax.dot_general(query, sink_keys, last_dims, preferred_element_type=jnp.float32)
                    * scale
                )
                scores = jnp.where(allowed, scores, -jnp.inf)
                sink_scores = jnp.where(sink_allowed, sink_scores, -jnp.inf)
                top = jnp.maximum(
                    jnp.max(scores, -1, keepdims=True), jnp.max(sink_scores, -1, keepdims=True)
                )
                near = jnp.exp(scores - top)
                far = jnp.exp(sink_scores - top)
                inverse = 1.0 / (
                    jnp.sum(near, -1, keepdims=True) + jnp.sum(far, -1, keepdims=True)
                )
                result = jnp.dot(
                    (near * inverse).astype(jnp.bfloat16),
                    near_values,
                    preferred_element_type=jnp.float32,
                ) + jnp.dot(
                    (far * inverse).astype(jnp.bfloat16),
                    sink_values,
                    preferred_element_type=jnp.float32,
                )
                mixed[step, :, part] = result.astype(jnp.bfloat16)

            @pl.when(step > 0)
            def _():
                to_half(step - 1, 1).start()

            @pl.when(step > 2)
            def _():
                to_half(step - 1, 0).start()

            @pl.when(step == 2)
            def _():
                for flip in range(2):
                    for i in range(2):
                        piece = passing.at[i, flip]
                        copy(passing_slot(flip, i), piece, piece, partner).wait_recv()
                        hand_on(flip, i).start()

            return carry

        lax.fori_loop(0, 8, attend, 0)
        own = pltpu.make_async_copy(mixed.at[7], context.at[dp, :, columns(q)], local.at[3])
        own.start()
        to_half(7, 1).start()

        def source_of(step):
            turn = step // 2
            return page_near(8 - FAR - turn * (turn + 1) // 2, 1 + step)

        def landed(step, half):
            return context.at[dp if half == 0 else 1 - dp, :, columns(source_of(step))]

        def pass_context(step):
            piece = landed(step, 1)
            return copy(step, piece, piece, partner)

        for step in range(2):
            copy(8 + step, landed(step, 1), landed(step, 1), partner).wait_recv()
            pass_context(step).start()
        for shift, flip in spread:
            source = page_near(4 - shift, flip)
            for i in range(2):
                piece = caches[i][1].at[source]
                copy(cache_slot(shift, flip, i), piece, piece, partner).wait_recv()
        for step in range(2, 8):
            copy(8 + step, landed(step, 1), landed(step, 1), partner).wait_recv()
        for step in range(7):
            copy(step, landed(step, 0), landed(step, 0), partner).wait_recv()
        for c in sent + [hand_on(flip, i) for flip in range(2) for i in range(2)]:
            c.wait_send()
        for c in own_copies[1:]:
            c.wait()
        for step in range(8):
            if step < 2:
                pass_context(step).wait_send()
            elif step < 7:
                to_half(step, 0).wait_send()
            to_half(step, 1).wait_send()
        own.wait()

    return send_cache, send_edges, attend_all


def mixed_pages(page, slab, note, gain, freq):
    rows, features = page.shape
    depth, columns = slab.shape
    block_rows = KEY_VALUE_HEADS * rows
    width = columns - 2 * HEAD_SIZE
    count = NSEG * SINKS
    vmem = pl.BlockSpec(memory_space=pltpu.VMEM)
    hbm = pl.BlockSpec(memory_space=pltpu.HBM)
    cache = jax.ShapeDtypeStruct((KEY_VALUE_HEADS, PAGE_ROWS, HEAD_SIZE), page.dtype)
    dtype = page.dtype
    return pl.pallas_call(
        kernel,
        out_shape=(
            jax.ShapeDtypeStruct((2, PAGE_ROWS, KEY_VALUE_HEADS * width), dtype),
            cache,
            cache,
        ),
        in_specs=[vmem] * 5,
        out_specs=(hbm,) * 3,
        scratch_shapes=[
            pltpu.VMEM((8, 2, 2, rows // 2, features), dtype),
            pltpu.VMEM((16, 2, 2, depth // 4, columns), slab.dtype),
            pltpu.VMEM((4, 4, 8, 1, note.shape[0]), note.dtype),
            pltpu.VMEM((2 * rows, features), dtype),
            pltpu.VMEM((block_rows, width), dtype),
            pltpu.VMEM((block_rows, 1), jnp.int32),
            pltpu.VMEM((2, count), jnp.int32),
            pltpu.VMEM((2, count, HEAD_SIZE), dtype),
            pltpu.VMEM((WINDOW + block_rows, HEAD_SIZE), dtype),
            pltpu.VMEM((WINDOW + block_rows, HEAD_SIZE), dtype),
            pltpu.VMEM((16, 2, count, HEAD_SIZE), dtype),
            pltpu.VMEM((8, PAGE_ROWS, width), dtype),
            pltpu.VMEM((2, 2, PAGE_ROWS, HEAD_SIZE), dtype),
            pltpu.SemaphoreType.DMA((COPIES,)),
            pltpu.SemaphoreType.DMA((COPIES,)),
            pltpu.SemaphoreType.DMA((3,)),
            pltpu.SemaphoreType.DMA((ATTEND_COPIES,)),
            pltpu.SemaphoreType.DMA((ATTEND_COPIES,)),
            pltpu.SemaphoreType.DMA((4,)),
        ],
        compiler_params=pltpu.CompilerParams(collective_id=0, has_side_effects=True),
        name="mixed_pages",
    )(
        page.reshape(2, rows // 2, features),
        slab.reshape(2, 2, depth // 4, columns),
        note.reshape(1, -1),
        gain.reshape(1, -1),
        freq.reshape(1, -1),
    )


def body(tokens, norm_gain, segments, deal_table, projection):
    group_id = lax.axis_index("dp")
    owner_group = jnp.sum(jnp.where(jnp.arange(deal_table.shape[1]) == group_id, deal_table[0], 0))
    client = jnp.where(owner_group == group_id, group_id, 1 - group_id).astype(jnp.int32)
    note = jnp.concatenate((segments[0], jnp.broadcast_to(client, segments[0].shape)))
    rope_freq = rope_base ** (-(jnp.arange(0, HEAD_SIZE, 2).astype(jnp.float32) / HEAD_SIZE))
    contexts, key_cache, value_cache = mixed_pages(
        tokens[0], projection, note, norm_gain, rope_freq
    )
    context = jnp.where(owner_group == 1, contexts[1], contexts[0])
    return (context[None], key_cache[None], value_cache[None])


def solution(mesh):
    placed = (P("dp", "tensor", None), P(), P("dp", "tensor"), P("tensor", None), P("tensor", None))
    return jax.shard_map(
        body,
        mesh=mesh,
        in_specs=placed,
        out_specs=(
            P("dp", "tensor", None),
            P("dp", None, "tensor", None),
            P("dp", None, "tensor", None),
        ),
        check_vma=False,
    )
```
